768 devices in a mesh: dp: 32 (over y, x), expert: 12 (over z), tensor: 2 (over core).
Axes of the slice: x: 4, y: 8, z: 12, core: 2. Of those that a mesh axis runs over, the one named last changes fastest.
Arguments:
- tokens: bfloat16 [49152, 2048], P(('dp', 'expert'), 'tensor'), may hold values from -6 to 6
- expert_ids: int32 [49152, 8], P(('dp', 'expert')), may hold values from 0 to 127, as said below
- route_weight: float32 [49152, 8], P(('dp', 'expert')), may hold values from 0.2 to 1
- gate_weight: bfloat16 [12, 2048, 768], P('expert', None, 'tensor'), may hold values from -0.125 to 0.125
- up_weight: bfloat16 [12, 2048, 768], P('expert', None, 'tensor'), may hold values from -0.125 to 0.125
- down_weight: bfloat16 [12, 768, 2048], P('expert', 'tensor'), may hold values from -0.21875 to 0.21875
- cotangent: bfloat16 [49152, 2048], P(('dp', 'expert'), 'tensor'), may hold values from -6 to 6
Outputs:
- mixed: bfloat16 [49152, 2048], P(('dp', 'expert'), 'tensor')
- token_grad: bfloat16 [49152, 2048], P(('dp', 'expert'), 'tensor')
- down_grad: bfloat16 [12, 768, 2048], P('expert', 'tensor', 'dp')
The draws below stay inside these ranges and needn't reach their ends.
Inputs may be any that keep to these rules, and one draw needn't show every extreme that they name: `expert_ids`: among the rows of one device, at most 12 pairs choose the same expert; in every replica some expert below 12 is chosen by exactly 12 pairs on each of the replica's 12 devices; a token's choices are distinct.
All inputs are finite; a program needn't handle non-finite values.
Results may differ from the reference program's by a relative error of at most 0.017.
Values may be sent and summed in bfloat16 or wider, within the bound.
No kernel may reach another device: no remote copies, remote signals or barrier semaphores. Data moves between devices by JAX's collectives and lax.ppermute only.
A program may use at most 32 MiB of HBM per device.

```python
import jax
import jax.numpy as jnp
from jax import lax

D = 2048
FF = 768
EXPERTS = 128
TOPK = 8
TOK_DEV = 128
WINDOW = 12
CAP = 12
TOKENS = 49152
N_DP = 32
N_TENSOR = 2


def draw_expert_ids(key, part):
    nblk = TOKENS // TOK_DEV
    nrep = nblk // WINDOW
    per_block = TOK_DEV * TOPK
    chosen = jax.random.randint(jax.random.fold_in(key, 11), (nrep,), 0, WINDOW, dtype=jnp.int32)
    fixed = jnp.repeat(chosen, WINDOW)
    experts_row = jnp.arange(EXPERTS, dtype=jnp.int32)[None, :]
    is_fixed = experts_row == fixed[:, None]
    levels = jax.random.randint(jax.random.fold_in(key, 12), (nblk, EXPERTS), 0, 5, dtype=jnp.int32)
    weights = jnp.where(is_fixed, 0, jnp.left_shift(jnp.ones_like(levels), levels))
    rest = per_block - CAP
    base = jnp.minimum(CAP, rest * weights // jnp.sum(weights, axis=1, keepdims=True))
    base = jnp.where(is_fixed, CAP, base)
    deficit = per_block - jnp.sum(base, axis=1, keepdims=True)
    room = CAP - base
    scores = jax.random.randint(jax.random.fold_in(key, 13), (nblk, EXPERTS), 0, 1 << 20, dtype=jnp.int32) * EXPERTS + experts_row
    order = jnp.argsort(scores, axis=1)
    room_perm = jnp.take_along_axis(room, order, axis=1)
    earlier = jnp.cumsum(room_perm, axis=1) - room_perm
    added_perm = jnp.clip(deficit - earlier, 0, room_perm)
    inverse = jnp.argsort(order, axis=1)
    counts = base + jnp.take_along_axis(added_perm, inverse, axis=1)
    ends = jnp.cumsum(counts, axis=1)
    position = jnp.arange(per_block, dtype=jnp.int32)
    sequence = jnp.sum((ends[:, None, :] <= position[None, :, None]).astype(jnp.int32), axis=2)
    grid = jnp.transpose(sequence.reshape(nblk, TOPK, TOK_DEV), (0, 2, 1))
    token_scores = jax.random.randint(jax.random.fold_in(key, 14), (nblk, TOK_DEV), 0, 1 << 20, dtype=jnp.int32) * TOK_DEV + jnp.arange(TOK_DEV, dtype=jnp.int32)[None, :]
    token_order = jnp.argsort(token_scores, axis=1)
    grid = jnp.take_along_axis(grid, token_order[:, :, None], axis=1)
    choice_scores = jax.random.randint(jax.random.fold_in(key, 15), (nblk, TOK_DEV, TOPK), 0, 1 << 20, dtype=jnp.int32) * TOPK + jnp.arange(TOPK, dtype=jnp.int32)[None, None, :]
    grid = jnp.take_along_axis(grid, jnp.argsort(choice_scores, axis=2), axis=2)
    return grid.reshape(TOKENS, TOPK).astype(jnp.int32)


def steps_of(key, dims, cuts, low, largest):
    def one(dim, shards_of):
        draws = jax.random.uniform(jax.random.fold_in(jax.random.fold_in(key, 6), dim), (shards_of,), jnp.float32, low / len(cuts), largest / len(cuts))
        return jnp.repeat(jnp.exp(draws), dims[dim] // shards_of).reshape((-1,) + (1,) * (len(dims) - dim - 1))

    loudness = one(*cuts[0])
    for cut in cuts[1:]:
        loudness = loudness * one(*cut)
    return loudness


def centred(own_key, extent, width, limit, split=(), held_as=jnp.bfloat16):
    level = steps_of(own_key, extent, split, -0.22, 0.18) if split else 1.0
    array = jax.random.normal(own_key, extent, jnp.float32) * width * level
    return jnp.minimum(jnp.maximum(array, -limit), limit).astype(held_as)


def setup_inputs(seed: int = 0) -> dict:
    keys = jax.random.split(jax.random.key(seed), 8)
    return {
        "tokens": centred(keys[0], (TOKENS, D), 1.0, 6.0, ((0, 384), (1, 2))),
        "expert_ids": draw_expert_ids(jax.random.fold_in(keys[7], 71), 0),
        "route_weight": jnp.clip(0.2 + 0.8 * jax.random.uniform(keys[2], (TOKENS, TOPK), jnp.float32) ** steps_of(keys[2], (TOKENS, TOPK), ((0, 384),), -0.2, 0.2), 0.2, 1.0),
        "gate_weight": centred(keys[3], (WINDOW, D, FF), D ** -0.5, 0.125, ((0, 12), (2, 2))),
        "up_weight": centred(keys[4], (WINDOW, D, FF), D ** -0.5, 0.125, ((0, 12), (2, 2))),
        "down_weight": centred(keys[5], (WINDOW, FF, D), FF ** -0.5, 0.21875, ((0, 12), (1, 2))),
        "cotangent": centred(keys[6], (TOKENS, D), 1.0, 6.0, ((0, 384), (1, 2))),
    }


def silu_parts(gate):
    sig = jax.nn.sigmoid(gate)
    return sig, gate * sig


def block_rounded(partials):
    return jnp.sum(partials.astype(jnp.bfloat16).astype(jnp.float32), axis=0)


def reference(tokens, expert_ids, route_weight, gate_weight, up_weight, down_weight, cotangent):
    nblk = TOKENS // TOK_DEV
    per_block = TOK_DEV * TOPK
    pairs_all = TOKENS * TOPK
    width_tp = FF // N_TENSOR
    flat_ids = expert_ids.reshape(nblk, per_block)
    onehot = (flat_ids[:, :, None] == jnp.arange(WINDOW, dtype=jnp.int32)[None, None, :]).astype(jnp.int32)
    before = jnp.cumsum(onehot, axis=1) - onehot
    rank = jnp.sum(before * onehot, axis=2).astype(jnp.int32)
    inside = flat_ids < WINDOW
    row_expert = jnp.where(inside, flat_ids, WINDOW).astype(jnp.int32)
    row_rank = jnp.where(inside, rank, 0).astype(jnp.int32)
    blocks = jnp.broadcast_to(jnp.arange(nblk, dtype=jnp.int32)[:, None], (nblk, per_block))
    pair_index = jnp.arange(pairs_all, dtype=jnp.int32).reshape(nblk, per_block)
    table = jnp.full((WINDOW + 1, nblk, CAP), pairs_all, jnp.int32).at[row_expert, blocks, row_rank].set(pair_index)[:WINDOW]
    x_pairs = jnp.concatenate([jnp.repeat(tokens, TOPK, axis=0), jnp.zeros((1, D), jnp.bfloat16)], axis=0)
    scaled = (jnp.repeat(cotangent.astype(jnp.float32), TOPK, axis=0) * route_weight.reshape(pairs_all, 1)).astype(jnp.bfloat16)
    g_pairs = jnp.concatenate([scaled, jnp.zeros((1, D), jnp.bfloat16)], axis=0)

    def one_expert(items):
        w_gate, w_up, w_down, tab = items
        idx = tab.reshape(nblk * CAP)
        x_rows = x_pairs[idx]
        grad_rows = g_pairs[idx]
        gate = jnp.dot(x_rows, w_gate, preferred_element_type=jnp.float32)
        up = jnp.dot(x_rows, w_up, preferred_element_type=jnp.float32)
        sig, act = silu_parts(gate)
        hidden = (act * up).astype(jnp.bfloat16)
        rows = nblk * CAP
        hid_blocks = hidden.astype(jnp.float32).reshape(rows, N_TENSOR, width_tp)
        down_blocks = w_down.astype(jnp.float32).reshape(N_TENSOR, width_tp, D)
        out_rows = block_rounded(jnp.einsum('rtf,tfd->trd', hid_blocks, down_blocks)).astype(jnp.bfloat16)
        hidden_grad = jnp.dot(grad_rows, w_down.T, preferred_element_type=jnp.float32)
        gate_term = (hidden_grad * up * sig * (1.0 + gate * (1.0 - sig))).astype(jnp.bfloat16)
        up_term = (hidden_grad * act).astype(jnp.bfloat16)
        gt = gate_term.astype(jnp.float32).reshape(rows, N_TENSOR, width_tp)
        ut = up_term.astype(jnp.float32).reshape(rows, N_TENSOR, width_tp)
        wg = w_gate.astype(jnp.float32).reshape(D, N_TENSOR, width_tp)
        wu = w_up.astype(jnp.float32).reshape(D, N_TENSOR, width_tp)
        parts = jnp.einsum('rtf,dtf->trd', gt, wg) + jnp.einsum('rtf,dtf->trd', ut, wu)
        row_grad = block_rounded(parts).astype(jnp.bfloat16)
        per_rep = rows // N_DP
        gr = grad_rows.astype(jnp.float32).reshape(N_DP, per_rep, D)
        hr = hidden.astype(jnp.float32).reshape(N_DP, per_rep, FF)
        g_down = block_rounded(jnp.einsum('rnf,rnd->rfd', hr, gr)).astype(jnp.bfloat16)
        return out_rows, row_grad, g_down

    out_rows, row_grad, down_grad = lax.map(one_expert, (gate_weight, up_weight, down_weight, table))
    flat_tab = table.reshape(WINDOW * nblk * CAP)
    out_pairs = jnp.zeros((pairs_all + 1, D), jnp.bfloat16).at[flat_tab].set(out_rows.reshape(-1, D))
    grad_pairs = jnp.zeros((pairs_all + 1, D), jnp.bfloat16).at[flat_tab].set(row_grad.reshape(-1, D))
    out_tok = out_pairs[:pairs_all].astype(jnp.float32).reshape(TOKENS, TOPK, D)
    mixed = jnp.sum(out_tok * route_weight[:, :, None], axis=1).astype(jnp.bfloat16)
    token_grad = jnp.sum(grad_pairs[:pairs_all].astype(jnp.float32).reshape(TOKENS, TOPK, D), axis=1).astype(jnp.bfloat16)
    return mixed, token_grad, down_grad
```

```python
import functools

import jax
import jax.numpy as jnp
from jax import lax
from jax.experimental import pallas as pl
from jax.experimental.pallas import tpu as pltpu
from jax.sharding import PartitionSpec as P

EXPERTS = 128
NX = 4
B16 = jnp.bfloat16
F32 = jnp.float32
ROWS0 = (((0,), (0,)), ((), ()))
COLS1 = (((1,), (1,)), ((), ()))


def dot(a, b, dims=None):
    if dims is None:
        dims = (((1,), (0,)), ((), ()))
    return lax.dot_general(a, b, dims, preferred_element_type=F32)


def fused(kernel, outs, *args, scalars=0, flops=0):
    specs = [pl.BlockSpec(memory_space=pltpu.SMEM)] * scalars
    specs += [pl.BlockSpec(memory_space=pltpu.VMEM)] * (len(args) - scalars)
    nbytes = sum(a.size * a.dtype.itemsize for a in list(args) + list(outs))
    return pl.pallas_call(
        kernel,
        out_shape=outs,
        in_specs=specs,
        out_specs=[pl.BlockSpec(memory_space=pltpu.VMEM)] * len(outs),
        cost_estimate=pl.CostEstimate(flops=flops, bytes_accessed=nbytes, transcendentals=0),
    )(*args)


def routing(ids_ref, w_ref, owners, cap):
    choose, toks = ids_ref.shape
    expert = lax.broadcasted_iota(jnp.int32, (owners, toks), 0)
    mask = jnp.zeros((owners, toks), F32)
    weight = jnp.zeros((owners, toks), F32)
    for k in range(choose):
        hit = ids_ref[k : k + 1, :] == expert
        mask = mask + jnp.where(hit, 1.0, 0.0)
        weight = weight + jnp.where(hit, w_ref[k : k + 1, :], 0.0)
    earlier = lax.broadcasted_iota(jnp.int32, (toks, toks), 0) < lax.broadcasted_iota(
        jnp.int32, (toks, toks), 1
    )
    rank = dot(mask.astype(B16), jnp.where(earlier, 1.0, 0.0).astype(B16))
    code = jnp.where(mask > 0.0, rank, -100.0)
    shape = (owners, 2 * cap, toks)
    code = jnp.broadcast_to(code[:, None, :], shape)
    weight = jnp.broadcast_to(weight[:, None, :], shape)
    row = lax.broadcasted_iota(jnp.int32, shape, 1).astype(F32)
    flat = (owners * 2 * cap, toks)
    left = jnp.where(code == row, 1.0, 0.0).reshape(flat)
    right = jnp.where(code == row - float(cap), 1.0, 0.0).reshape(flat)
    return left, right, weight.reshape(flat)


def dispatch_kernel(owners, cap, ids_ref, w_ref, tok_ref, cot_ref, out_ref):
    left, right, weight = routing(ids_ref, w_ref, owners, cap)
    scale = jnp.sum(right * weight, axis=1, keepdims=True)
    rows = dot(left.astype(B16), tok_ref[...]) + dot(right.astype(B16), cot_ref[...]) * scale
    out_ref[...] = rows.astype(B16)


def plan_kernel(owners, cap, ids_ref, w_ref, high_ref, low_ref, right_ref):
    left, right, weight = routing(ids_ref, w_ref, owners, cap)
    left = (left * weight).T
    high = left.astype(B16)
    high_ref[...] = high
    low_ref[...] = (left - high.astype(F32)).astype(B16)
    right_ref[...] = right.T.astype(B16)


def combine_kernel(high_ref, low_ref, right_ref, rows_ref, mixed_ref, grad_ref):
    rows = rows_ref[...]
    mixed_ref[...] = (dot(high_ref[...], rows) + dot(low_ref[...], rows)).astype(B16)
    grad_ref[...] = dot(right_ref[...], rows).astype(B16)


def pick(shape, axis, cap, shift):
    compact = lax.broadcasted_iota(jnp.int32, shape, axis).astype(F32)
    chunk = lax.broadcasted_iota(jnp.int32, shape, 1 - axis).astype(F32)
    block = jnp.floor((compact + 0.5) * (1.0 / cap))
    return jnp.where(chunk == compact + cap * block + shift, 1.0, 0.0).astype(B16)


def expert_kernel(
    cap, where_ref, own_ref, oth_ref, wg_ref, wu_ref, wd_ref, keep_ref, give_ref, pack_ref
):
    side, x = where_ref[0], where_ref[1]
    rows, half = own_ref.shape
    slots = rows // 2
    here = pl.ds(pl.multiple_of(side * half, half), half)
    there = pl.ds(pl.multiple_of((1 - side) * half, half), half)
    own, oth = own_ref[...], oth_ref[...]
    to_x = pick((slots, rows), 0, cap, 0)
    to_g = pick((slots, rows), 0, cap, cap)
    x_own, x_oth = dot(to_x, own).astype(B16), dot(to_x, oth).astype(B16)
    g_own, g_oth = dot(to_g, own).astype(B16), dot(to_g, oth).astype(B16)
    wg_own, wg_oth = wg_ref[here, :], wg_ref[there, :]
    wu_own, wu_oth = wu_ref[here, :], wu_ref[there, :]
    wd_own, wd_oth = wd_ref[:, here], wd_ref[:, there]
    gate = dot(x_own, wg_own) + dot(x_oth, wg_oth)
    up = dot(x_own, wu_own) + dot(x_oth, wu_oth)
    sig = 1.0 / (1.0 + jnp.exp(-gate))
    act = gate * sig
    hidden = (act * up).astype(B16)
    hidden_grad = dot(g_own, wd_own, COLS1) + dot(g_oth, wd_oth, COLS1)
    gate_term = (hidden_grad * up * sig * (1.0 + gate * (1.0 - sig))).astype(B16)
    up_term = (hidden_grad * act).astype(B16)
    from_x = pick((rows, slots), 1, cap, 0)
    from_g = pick((rows, slots), 1, cap, cap)
    for wd, wg, wu, out in (
        (wd_oth, wg_oth, wu_oth, give_ref),
        (wd_own, wg_own, wu_own, keep_ref),
    ):
        out_rows = dot(hidden, wd).astype(B16)
        row_grad = (dot(gate_term, wg, COLS1) + dot(up_term, wu, COLS1)).astype(B16)
        out[...] = (dot(from_x, out_rows) + dot(from_g, row_grad)).astype(B16)
    wide = half // 2
    nyh = half // (64 * NX)
    for s, g in ((side, g_own), (1 - side, g_oth)):
        for xd in range(NX):
            slot = lax.rem(xd - x + NX, NX)
            for par in range(2):
                cols = jnp.concatenate(
                    [g[:, (y * NX + xd) * 64 : (y * NX + xd) * 64 + 64] for y in range(par, nyh, 2)],
                    axis=1,
                )
                n = cols.shape[1]
                pack_ref[slot, :, pl.ds(pl.multiple_of(par * (wide // 2) + s * n, 128), n)] = cols
    for k in range(NX):
        pack_ref[k, :, wide:] = hidden


def down_kernel(where_ref, p0, p1, p2, p3, keep_ref, give_ref):
    par = where_ref[0]
    n = keep_ref.shape[0]
    wide = 2 * n
    mine = pl.ds(pl.multiple_of(par * n, n), n)
    theirs = pl.ds(pl.multiple_of((1 - par) * n, n), n)
    for cols, out in ((theirs, give_ref), (mine, keep_ref)):
        total = None
        for p in (p0, p1, p2, p3):
            part = dot(p[:, cols], p[:, wide:], ROWS0)
            total = part if total is None else total + part
        out[...] = total.astype(B16)


def spread_kernel(where_ref, a_ref, b_ref, own_ref, s1_ref, s2_ref, s3_ref):
    q = where_ref[0]
    n = own_ref.shape[0]
    for k, out in enumerate((own_ref, s1_ref, s2_ref, s3_ref)):
        rows = pl.ds(pl.multiple_of(lax.rem(q + k, 4) * n, n), n)
        out[...] = (a_ref[rows, :].astype(F32) + b_ref[rows, :].astype(F32)).astype(B16)


def per_device(tokens, expert_ids, route_weight, gate_weight, up_weight, down_weight, cotangent):
    owners = lax.axis_size("expert")
    n_dp = lax.axis_size("dp")
    ny = n_dp // NX
    tok_rows, choose = expert_ids.shape
    cap = 3 * tok_rows * choose // (2 * EXPERTS)
    half = tokens.shape[1]
    slots = owners * cap
    ff = gate_weight.shape[2]
    bf = lambda *shape: jax.ShapeDtypeStruct(shape, B16)
    side = lax.axis_index("tensor").astype(jnp.int32)
    dp = lax.axis_index("dp").astype(jnp.int32)
    x, y = dp % NX, dp // NX
    ids_t, w_t = expert_ids.T, route_weight.T
    (send,) = fused(
        functools.partial(dispatch_kernel, owners, cap),
        [bf(2 * slots, half)],
        ids_t,
        w_t,
        tokens,
        cotangent,
        flops=4 * slots * tok_rows * half * 2,
    )
    high, low, right = fused(
        functools.partial(plan_kernel, owners, cap),
        [bf(tok_rows, 2 * slots)] * 3,
        ids_t,
        w_t,
        flops=tok_rows**3,
    )

    def trade(rows):
        chunks = rows.reshape(owners, 2 * cap, half)
        chunks = lax.all_to_all(chunks, "expert", split_axis=0, concat_axis=0, tiled=True)
        return chunks.reshape(2 * slots, half)

    def swap(v):
        return lax.ppermute(v, "tensor", [(0, 1), (1, 0)])

    def to_x(v, k):
        pairs = [(b * NX + a, b * NX + (a + k) % NX) for b in range(ny) for a in range(NX)]
        return lax.ppermute(v, "dp", pairs)

    def to_y(v, move):
        return lax.ppermute(v, "dp", [(b * NX + a, move(b) * NX + a) for b in range(ny) for a in range(NX)])

    own = trade(send)
    oth = swap(own)
    keep, give, pack = fused(
        functools.partial(expert_kernel, cap),
        [bf(2 * slots, half), bf(2 * slots, half), bf(NX, slots, half // 2 + ff)],
        jnp.stack([side, x]),
        own,
        oth,
        gate_weight[0],
        up_weight[0],
        down_weight[0],
        scalars=1,
        flops=slots * half * 2 * ff * 12 + slots * 2 * slots * half * 20,
    )
    total = (keep.astype(F32) + swap(give).astype(F32)).astype(B16)
    back = trade(total)
    mixed, token_grad = fused(
        combine_kernel,
        [bf(tok_rows, half)] * 2,
        high,
        low,
        right,
        back,
        flops=tok_rows * 2 * slots * half * 6,
    )
    parts = [pack[0]] + [to_x(pack[k], k) for k in range(1, NX)]
    n = half // (2 * NX)
    down_keep, down_give = fused(
        down_kernel,
        [bf(half // 4, ff)] * 2,
        (y % 2).reshape(1),
        *parts,
        scalars=1,
        flops=half // 2 * ff * slots * 2 * NX,
    )
    down_got = to_y(down_give, lambda b: b ^ 1)
    mine, *sends = fused(
        spread_kernel,
        [bf(half // 16, ff)] * 4,
        (y // 2).reshape(1),
        down_keep,
        down_got,
        scalars=1,
    )
    down = mine.astype(F32)
    for k, s in enumerate(sends, 1):
        down = down + to_y(s, lambda b, k=k: (b + 2 * k) % ny).astype(F32)
    return mixed, token_grad, down.astype(B16).T[None]


def solution(mesh):
    placed = (
        P(("dp", "expert"), "tensor"),
        P(("dp", "expert"), None),
        P(("dp", "expert"), None),
        P("expert", None, "tensor"),
        P("expert", None, "tensor"),
        P("expert", "tensor", None),
        P(("dp", "expert"), "tensor"),
    )
    return jax.shard_map(
        per_device,
        mesh=mesh,
        in_specs=placed,
        out_specs=(
            P(("dp", "expert"), "tensor"),
            P(("dp", "expert"), "tensor"),
            P("expert", "tensor", "dp"),
        ),
        check_vma=False,
    )
```

```python
import functools
import math

import jax
import jax.numpy as jnp
from jax import lax
from jax.experimental import pallas as pl
from jax.experimental.pallas import tpu as pltpu
from jax.sharding import PartitionSpec as P

EXPERTS = 128
NX = 4
B16 = jnp.bfloat16
F32 = jnp.float32
ROWS0 = (((0,), (0,)), ((), ()))
COLS1 = (((1,), (1,)), ((), ()))


def dot(a, b, dims=None):
    if dims is None:
        dims = (((1,), (0,)), ((), ()))
    return lax.dot_general(a, b, dims, preferred_element_type=F32)


def hbm(v):
    return pltpu.with_memory_space_constraint(v, pltpu.HBM)


def fused(kernel, outs, *args, scalars=0, flops=0, mib=8):
    specs = [pl.BlockSpec(memory_space=pltpu.SMEM)] * scalars
    specs += [pl.BlockSpec(memory_space=pltpu.VMEM)] * (len(args) - scalars)
    nbytes = sum(math.prod(a.shape) * a.dtype.itemsize for a in list(args) + list(outs))
    return pl.pallas_call(
        kernel,
        out_shape=outs,
        in_specs=specs,
        out_specs=[pl.BlockSpec(memory_space=pltpu.VMEM)] * len(outs),
        compiler_params=pltpu.CompilerParams(vmem_limit_bytes=mib << 20),
        cost_estimate=pl.CostEstimate(flops=flops, bytes_accessed=nbytes, transcendentals=0),
    )(*args)


def routing(ids_ref, w_ref, owners, cap):
    choose, toks = ids_ref.shape
    expert = lax.broadcasted_iota(jnp.int32, (owners, toks), 0)
    mask = jnp.zeros((owners, toks), F32)
    weight = jnp.zeros((owners, toks), F32)
    for k in range(choose):
        hit = ids_ref[k : k + 1, :] == expert
        mask = mask + jnp.where(hit, 1.0, 0.0)
        weight = weight + jnp.where(hit, w_ref[k : k + 1, :], 0.0)
    earlier = lax.broadcasted_iota(jnp.int32, (toks, toks), 0) < lax.broadcasted_iota(
        jnp.int32, (toks, toks), 1
    )
    rank = dot(mask.astype(B16), jnp.where(earlier, 1.0, 0.0).astype(B16))
    code = jnp.where(mask > 0.0, rank, -100.0)
    shape = (owners, 2 * cap, toks)
    code = jnp.broadcast_to(code[:, None, :], shape)
    weight = jnp.broadcast_to(weight[:, None, :], shape)
    row = lax.broadcasted_iota(jnp.int32, shape, 1).astype(F32)
    flat = (owners * 2 * cap, toks)
    left = jnp.where(code == row, 1.0, 0.0).reshape(flat)
    right = jnp.where(code == row - float(cap), 1.0, 0.0).reshape(flat)
    return left, right, weight.reshape(flat)


def dispatch_kernel(owners, cap, ids_ref, w_ref, tok_ref, cot_ref, out_ref):
    left, right, weight = routing(ids_ref, w_ref, owners, cap)
    scale = jnp.sum(right * weight, axis=1, keepdims=True)
    rows = dot(left.astype(B16), tok_ref[...]) + dot(right.astype(B16), cot_ref[...]) * scale
    out_ref[...] = rows.astype(B16)


def plan_kernel(owners, cap, ids_ref, w_ref, high_ref, low_ref, right_ref):
    left, right, weight = routing(ids_ref, w_ref, owners, cap)
    left = (left * weight).T
    high = left.astype(B16)
    high_ref[...] = high
    low_ref[...] = (left - high.astype(F32)).astype(B16)
    right_ref[...] = right.T.astype(B16)


def combine_kernel(high_ref, low_ref, right_ref, rows_ref, mixed_ref, grad_ref):
    rows = rows_ref[...]
    mixed_ref[...] = (dot(high_ref[...], rows) + dot(low_ref[...], rows)).astype(B16)
    grad_ref[...] = dot(right_ref[...], rows).astype(B16)


def pick(shape, axis, cap, shift):
    compact = lax.broadcasted_iota(jnp.int32, shape, axis).astype(F32)
    chunk = lax.broadcasted_iota(jnp.int32, shape, 1 - axis).astype(F32)
    block = jnp.floor((compact + 0.5) * (1.0 / cap))
    return jnp.where(chunk == compact + cap * block + shift, 1.0, 0.0).astype(B16)


def halves(side_ref, half):
    side = side_ref[0]
    here = pl.ds(pl.multiple_of(side * half, half), half)
    there = pl.ds(pl.multiple_of((1 - side) * half, half), half)
    return side, here, there


def forward_kernel(cap, side_ref, own_ref, oth_ref, wg_ref, wu_ref, gate_ref, up_ref, pack_ref):
    rows, half = own_ref.shape
    slots = rows // 2
    side, here, there = halves(side_ref, half)
    own, oth = own_ref[...], oth_ref[...]
    to_x = pick((slots, rows), 0, cap, 0)
    x_own, x_oth = dot(to_x, own).astype(B16), dot(to_x, oth).astype(B16)
    gate = dot(x_own, wg_ref[here, :]) + dot(x_oth, wg_ref[there, :])
    up = dot(x_own, wu_ref[here, :]) + dot(x_oth, wu_ref[there, :])
    hidden = (gate * (1.0 / (1.0 + jnp.exp(-gate))) * up).astype(B16)
    gate_ref[...] = gate
    up_ref[...] = up
    to_g = pick((slots, rows), 0, cap, cap)
    wide = half // 2
    nyh = half // (64 * NX)
    for s, rows_in in ((side, own), (1 - side, oth)):
        g = dot(to_g, rows_in).astype(B16)
        for xd in range(NX):
            for par in range(2):
                cols = jnp.concatenate(
                    [g[:, (y * NX + xd) * 64 : (y * NX + xd) * 64 + 64] for y in range(par, nyh, 2)],
                    axis=1,
                )
                n = cols.shape[1]
                pack_ref[xd, :, pl.ds(pl.multiple_of(par * (wide // 2) + s * n, 128), n)] = cols
    for xd in range(NX):
        pack_ref[xd, :, wide:] = hidden


def backward_kernel(
    cap, side_ref, own_ref, oth_ref, gate_ref, up_ref, wg_ref, wu_ref, wd_ref, keep_ref, give_ref
):
    rows, half = own_ref.shape
    slots = rows // 2
    _, here, there = halves(side_ref, half)
    to_g = pick((slots, rows), 0, cap, cap)
    g_own, g_oth = dot(to_g, own_ref[...]).astype(B16), dot(to_g, oth_ref[...]).astype(B16)
    gate, up = gate_ref[...], up_ref[...]
    sig = 1.0 / (1.0 + jnp.exp(-gate))
    act = gate * sig
    hidden = (act * up).astype(B16)
    hidden_grad = dot(g_own, wd_ref[:, here], COLS1) + dot(g_oth, wd_ref[:, there], COLS1)
    gate_term = (hidden_grad * up * sig * (1.0 + gate * (1.0 - sig))).astype(B16)
    up_term = (hidden_grad * act).astype(B16)
    from_x = pick((rows, slots), 1, cap, 0)
    from_g = pick((rows, slots), 1, cap, cap)
    for part, out in ((there, give_ref), (here, keep_ref)):
        out_rows = dot(hidden, wd_ref[:, part]).astype(B16)
        row_grad = dot(gate_term, wg_ref[part, :], COLS1) + dot(up_term, wu_ref[part, :], COLS1)
        out[...] = (dot(from_x, out_rows) + dot(from_g, row_grad.astype(B16))).astype(B16)


def down_kernel(part_ref, packs_ref, out_ref):
    n = out_ref.shape[0]
    cols = pl.ds(pl.multiple_of(part_ref[0] * n, n), n)
    total = None
    for k in range(NX):
        part = dot(packs_ref[k, :, cols], packs_ref[k, :, 2 * n :], ROWS0)
        total = part if total is None else total + part
    out_ref[...] = total.astype(B16)


def spread_kernel(where_ref, a_ref, b_ref, own_ref, s1_ref, s2_ref, s3_ref):
    q = where_ref[0]
    n = own_ref.shape[0]
    for k, out in enumerate((own_ref, s1_ref, s2_ref, s3_ref)):
        rows = pl.ds(pl.multiple_of(lax.rem(q + k, 4) * n, n), n)
        out[...] = (a_ref[rows, :].astype(F32) + b_ref[rows, :].astype(F32)).astype(B16)


def per_device(tokens, expert_ids, route_weight, gate_weight, up_weight, down_weight, cotangent):
    owners = lax.axis_size("expert")
    ny = lax.axis_size("y")
    tok_rows, choose = expert_ids.shape
    cap = 3 * tok_rows * choose // (2 * EXPERTS)
    half = tokens.shape[1]
    slots = owners * cap
    ff = gate_weight.shape[2]
    bf = lambda *shape: jax.ShapeDtypeStruct(shape, B16)
    side = lax.axis_index("tensor").astype(jnp.int32).reshape(1)
    y = lax.axis_index("y").astype(jnp.int32).reshape(1)
    ids_t, w_t = expert_ids.T, route_weight.T
    (send,) = fused(
        functools.partial(dispatch_kernel, owners, cap),
        [bf(2 * slots, half)],
        hbm(ids_t),
        hbm(w_t),
        hbm(tokens),
        hbm(cotangent),
        flops=4 * slots * tok_rows * half * 2,
    )
    high, low, right = fused(
        functools.partial(plan_kernel, owners, cap),
        [bf(tok_rows, 2 * slots)] * 3,
        hbm(ids_t),
        hbm(w_t),
        flops=tok_rows**3,
    )

    def trade(rows, axis, *shape):
        return lax.all_to_all(rows.reshape(shape), axis, split_axis=0, concat_axis=0, tiled=True)

    def swap(v):
        return lax.ppermute(v, "tensor", [(0, 1), (1, 0)])

    def to_y(v, move):
        return lax.ppermute(v, "y", [(b, move(b)) for b in range(ny)])

    chunks = (owners, 2 * cap, half)
    own = trade(send, "expert", *chunks).reshape(2 * slots, half)
    oth = swap(own)
    gate, up, pack = fused(
        functools.partial(forward_kernel, cap),
        [pltpu.HBM((slots, ff), F32)] * 2
        + [pltpu.HBM((NX, slots, half // 2 + ff), B16)],
        side,
        own,
        oth,
        gate_weight[0],
        hbm(up_weight[0]),
        scalars=1,
        flops=slots * half * 2 * ff * 4 + slots * 2 * slots * half * 8,
        mib=20,
    )
    packs = trade(pack, "x", *pack.shape)
    keep, give = fused(
        functools.partial(backward_kernel, cap),
        [bf(2 * slots, half)] * 2,
        side,
        own,
        oth,
        gate,
        up,
        hbm(gate_weight[0]),
        hbm(up_weight[0]),
        hbm(down_weight[0]),
        scalars=1,
        flops=slots * half * 2 * ff * 8 + slots * 2 * slots * half * 12,
        mib=24,
    )
    total = (keep.astype(F32) + swap(give).astype(F32)).astype(B16)
    back = trade(total, "expert", *chunks).reshape(2 * slots, half)
    mixed, token_grad = fused(
        combine_kernel,
        [bf(tok_rows, half)] * 2,
        high,
        low,
        right,
        back,
        flops=tok_rows * 2 * slots * half * 6,
    )
    down = functools.partial(
        fused, down_kernel, [bf(half // 4, ff)], scalars=1, flops=half // 4 * ff * slots * 2 * NX
    )
    (down_give,) = down(1 - y % 2, packs)
    down_got = to_y(down_give, lambda b: b ^ 1)
    (down_keep,) = down(y % 2, packs)
    mine, *sends = fused(
        spread_kernel, [bf(half // 16, ff)] * 4, y // 2, down_keep, down_got, scalars=1
    )
    total_down = mine.astype(F32)
    for k, s in enumerate(sends, 1):
        total_down = total_down + to_y(s, lambda b, k=k: (b + 2 * k) % ny).astype(F32)
    return mixed, token_grad, total_down.astype(B16).T[None]


def solution(mesh):
    dp, owners, tensor = (mesh.shape[a] for a in ("dp", "expert", "tensor"))
    mesh = jax.sharding.Mesh(
        mesh.devices.reshape(dp // NX, NX, owners, tensor), ("y", "x", "expert", "tensor")
    )
    blocks = ("y", "x", "expert")
    placed = (
        P(blocks, "tensor"),
        P(blocks, None),
        P(blocks, None),
        P("expert", None, "tensor"),
        P("expert", None, "tensor"),
        P("expert", "tensor", None),
        P(blocks, "tensor"),
    )

    return jax.shard_map(
        per_device,
        mesh=mesh,
        in_specs=placed,
        out_specs=(P(blocks, "tensor"), P(blocks, "tensor"), P("expert", "tensor", ("y", "x"))),
        check_vma=False,
    )
```

```python
import functools
import math

import jax
import jax.numpy as jnp
from jax import lax
from jax.experimental import pallas as pl
from jax.experimental.pallas import tpu as pltpu
from jax.sharding import PartitionSpec as P

EXPERTS = 128
NX = 4
B16 = jnp.bfloat16
F32 = jnp.float32
ROWS0 = (((0,), (0,)), ((), ()))
COLS1 = (((1,), (1,)), ((), ()))


def dot(a, b, dims=None):
    if dims is None:
        dims = (((1,), (0,)), ((), ()))
    return lax.dot_general(a, b, dims, preferred_element_type=F32)


def hbm(v):
    return pltpu.with_memory_space_constraint(v, pltpu.HBM)


def fused(kernel, outs, *args, scalars=0, flops=0, mib=8):
    specs = [pl.BlockSpec(memory_space=pltpu.SMEM)] * scalars
    specs += [pl.BlockSpec(memory_space=pltpu.VMEM)] * (len(args) - scalars)
    nbytes = sum(math.prod(a.shape) * a.dtype.itemsize for a in list(args) + list(outs))
    return pl.pallas_call(
        kernel,
        out_shape=outs,
        in_specs=specs,
        out_specs=[pl.BlockSpec(memory_space=pltpu.VMEM)] * len(outs),
        compiler_params=pltpu.CompilerParams(vmem_limit_bytes=mib << 20),
        cost_estimate=pl.CostEstimate(flops=flops, bytes_accessed=nbytes, transcendentals=0),
    )(*args)


def routing(ids_ref, w_ref, owners, cap):
    choose, toks = ids_ref.shape
    expert = lax.broadcasted_iota(jnp.int32, (owners, toks), 0)
    mask = jnp.zeros((owners, toks), F32)
    weight = jnp.zeros((owners, toks), F32)
    for k in range(choose):
        hit = ids_ref[k : k + 1, :] == expert
        mask = mask + jnp.where(hit, 1.0, 0.0)
        weight = weight + jnp.where(hit, w_ref[k : k + 1, :], 0.0)
    earlier = lax.broadcasted_iota(jnp.int32, (toks, toks), 0) < lax.broadcasted_iota(
        jnp.int32, (toks, toks), 1
    )
    rank = dot(mask.astype(B16), jnp.where(earlier, 1.0, 0.0).astype(B16))
    code = jnp.where(mask > 0.0, rank, -100.0)
    shape = (owners, 2 * cap, toks)
    code = jnp.broadcast_to(code[:, None, :], shape)
    weight = jnp.broadcast_to(weight[:, None, :], shape)
    row = lax.broadcasted_iota(jnp.int32, shape, 1).astype(F32)
    flat = (owners * 2 * cap, toks)
    left = jnp.where(code == row, 1.0, 0.0).reshape(flat)
    right = jnp.where(code == row - float(cap), 1.0, 0.0).reshape(flat)
    return left, right, weight.reshape(flat)


def dispatch_kernel(owners, cap, ids_ref, w_ref, tok_ref, cot_ref, out_ref):
    left, right, weight = routing(ids_ref, w_ref, owners, cap)
    scale = jnp.sum(right * weight, axis=1, keepdims=True)
    rows = dot(left.astype(B16), tok_ref[...]) + dot(right.astype(B16), cot_ref[...]) * scale
    out_ref[...] = rows.astype(B16)


def plan_kernel(owners, cap, ids_ref, w_ref, high_ref, low_ref, right_ref):
    left, right, weight = routing(ids_ref, w_ref, owners, cap)
    left = (left * weight).T
    high = left.astype(B16)
    high_ref[...] = high
    low_ref[...] = (left - high.astype(F32)).astype(B16)
    right_ref[...] = right.T.astype(B16)


def combine_kernel(high_ref, low_ref, right_ref, rows_ref, mixed_ref, grad_ref):
    rows = rows_ref[...]
    mixed_ref[...] = (dot(high_ref[...], rows) + dot(low_ref[...], rows)).astype(B16)
    grad_ref[...] = dot(right_ref[...], rows).astype(B16)


def pick(shape, axis, cap, shift):
    compact = lax.broadcasted_iota(jnp.int32, shape, axis).astype(F32)
    chunk = lax.broadcasted_iota(jnp.int32, shape, 1 - axis).astype(F32)
    block = jnp.floor((compact + 0.5) * (1.0 / cap))
    return jnp.where(chunk == compact + cap * block + shift, 1.0, 0.0).astype(B16)


def halves(side_ref, half):
    side = side_ref[0]
    here = pl.ds(pl.multiple_of(side * half, half), half)
    there = pl.ds(pl.multiple_of((1 - side) * half, half), half)
    return side, here, there


def forward_kernel(cap, side_ref, own_ref, oth_ref, wg_ref, wu_ref, gate_ref, up_ref, pack_ref):
    rows, half = own_ref.shape
    slots = rows // 2
    _, here, there = halves(side_ref, half)
    own, oth = own_ref[...], oth_ref[...]
    to_x = pick((slots, rows), 0, cap, 0)
    x_own, x_oth = dot(to_x, own).astype(B16), dot(to_x, oth).astype(B16)
    gate = dot(x_own, wg_ref[here, :]) + dot(x_oth, wg_ref[there, :])
    up = dot(x_own, wu_ref[here, :]) + dot(x_oth, wu_ref[there, :])
    hidden = (gate * (1.0 / (1.0 + jnp.exp(-gate))) * up).astype(B16)
    gate_ref[...] = gate
    up_ref[...] = up
    g = dot(pick((slots, rows), 0, cap, cap), own).astype(B16)
    wide = half // NX
    nyh = wide // 64
    for xd in range(NX):
        cols = [g[:, (y * NX + xd) * 64 : (y * NX + xd) * 64 + 64] for y in range(nyh)]
        pack_ref[xd, :, 0 : wide // 2] = jnp.concatenate(cols[0::2], axis=1)
        pack_ref[xd, :, wide // 2 : wide] = jnp.concatenate(cols[1::2], axis=1)
        pack_ref[xd, :, wide:] = hidden


def backward_kernel(
    cap, side_ref, own_ref, oth_ref, gate_ref, up_ref, wg_ref, wu_ref, wd_ref, keep_ref, give_ref
):
    rows, half = own_ref.shape
    slots = rows // 2
    _, here, there = halves(side_ref, half)
    to_g = pick((slots, rows), 0, cap, cap)
    g_own, g_oth = dot(to_g, own_ref[...]).astype(B16), dot(to_g, oth_ref[...]).astype(B16)
    gate, up = gate_ref[...], up_ref[...]
    sig = 1.0 / (1.0 + jnp.exp(-gate))
    act = gate * sig
    hidden = (act * up).astype(B16)
    hidden_grad = dot(g_own, wd_ref[:, here], COLS1) + dot(g_oth, wd_ref[:, there], COLS1)
    gate_term = (hidden_grad * up * sig * (1.0 + gate * (1.0 - sig))).astype(B16)
    up_term = (hidden_grad * act).astype(B16)
    from_x = pick((rows, slots), 1, cap, 0)
    from_g = pick((rows, slots), 1, cap, cap)
    for part, out in ((there, give_ref), (here, keep_ref)):
        out_rows = dot(hidden, wd_ref[:, part]).astype(B16)
        row_grad = dot(gate_term, wg_ref[part, :], COLS1) + dot(up_term, wu_ref[part, :], COLS1)
        out[...] = (dot(from_x, out_rows) + dot(from_g, row_grad.astype(B16))).astype(B16)


def down_kernel(bit_ref, side_ref, packs_ref, oth_ref, out_ref):
    n = out_ref.shape[0] // 2
    wide = oth_ref.shape[2]
    cols = pl.ds(pl.multiple_of(bit_ref[0] * n, n), n)
    side = side_ref[0]
    for ref, place in ((packs_ref, side), (oth_ref, 1 - side)):
        total = None
        for k in range(NX):
            part = dot(ref[k, :, cols], packs_ref[k, :, wide:], ROWS0)
            total = part if total is None else total + part
        out_ref[pl.ds(pl.multiple_of(place * n, n), n), :] = total.astype(B16)


def halve_kernel(blocks, bit_ref, a_ref, b_ref, keep_ref, give_ref):
    n = keep_ref.shape[0] // blocks
    bit = bit_ref[0]
    for at, out in ((1 - bit, give_ref), (bit, keep_ref)):
        for k in range(blocks):
            rows = pl.ds(pl.multiple_of((2 * k + at) * n, n), n)
            both = a_ref[rows, :].astype(F32) + b_ref[rows, :].astype(F32)
            out[k * n : (k + 1) * n, :] = both.astype(B16)


def per_device(tokens, expert_ids, route_weight, gate_weight, up_weight, down_weight, cotangent):
    owners = lax.axis_size("expert")
    ny = lax.axis_size("y")
    tok_rows, choose = expert_ids.shape
    cap = 3 * tok_rows * choose // (2 * EXPERTS)
    half = tokens.shape[1]
    slots = owners * cap
    ff = gate_weight.shape[2]
    bf = lambda *shape: jax.ShapeDtypeStruct(shape, B16)
    side = lax.axis_index("tensor").astype(jnp.int32).reshape(1)
    y = lax.axis_index("y").astype(jnp.int32).reshape(1)
    ids_t, w_t = expert_ids.T, route_weight.T
    (send,) = fused(
        functools.partial(dispatch_kernel, owners, cap),
        [bf(2 * slots, half)],
        hbm(ids_t),
        hbm(w_t),
        hbm(tokens),
        hbm(cotangent),
        flops=4 * slots * tok_rows * half * 2,
    )
    high, low, right = fused(
        functools.partial(plan_kernel, owners, cap),
        [bf(tok_rows, 2 * slots)] * 3,
        hbm(ids_t),
        hbm(w_t),
        flops=tok_rows**3,
    )

    def trade(rows, axis, *shape):
        return lax.all_to_all(rows.reshape(shape), axis, split_axis=0, concat_axis=0, tiled=True)

    def swap(v):
        return lax.ppermute(v, "tensor", [(0, 1), (1, 0)])

    def to_y(v, move):
        return lax.ppermute(v, "y", [(b, move(b)) for b in range(ny)])

    chunks = (owners, 2 * cap, half)
    own = trade(send, "expert", *chunks).reshape(2 * slots, half)
    oth = swap(own)
    gate, up, pack = fused(
        functools.partial(forward_kernel, cap),
        [pltpu.HBM((slots, ff), F32)] * 2
        + [pltpu.HBM((NX, slots, half // NX + ff), B16)],
        side,
        own,
        oth,
        gate_weight[0],
        hbm(up_weight[0]),
        scalars=1,
        flops=slots * half * 2 * ff * 4 + slots * 2 * slots * half * 8,
        mib=20,
    )
    packs = trade(pack, "x", *pack.shape)
    keep, give = fused(
        functools.partial(backward_kernel, cap),
        [bf(2 * slots, half)] * 2,
        side,
        own,
        oth,
        gate,
        up,
        hbm(gate_weight[0]),
        hbm(up_weight[0]),
        hbm(down_weight[0]),
        scalars=1,
        flops=slots * half * 2 * ff * 8 + slots * 2 * slots * half * 12,
        mib=24,
    )
    total = (keep.astype(F32) + swap(give).astype(F32)).astype(B16)
    back = trade(total, "expert", *chunks).reshape(2 * slots, half)
    mixed, token_grad = fused(
        combine_kernel,
        [bf(tok_rows, half)] * 2,
        high,
        low,
        right,
        back,
        flops=tok_rows * 2 * slots * half * 6,
    )
    cols_oth = swap(packs[:, :, : half // NX])
    down = functools.partial(
        fused, down_kernel, [bf(half // 4, ff)], scalars=2, flops=half // 4 * ff * slots * 2 * NX
    )
    bits = [y % 2, y // 2 % 2, y // 4]
    (give,) = down(1 - bits[0], side, packs, cols_oth)
    got = to_y(give, lambda b: b ^ 1)
    (keep,) = down(bits[0], side, packs, cols_oth)
    for step, blocks in ((1, 2), (2, 1)):
        rows = keep.shape[0] // 2
        keep, give = fused(
            functools.partial(halve_kernel, blocks),
            [bf(rows, ff)] * 2,
            bits[step],
            keep,
            got,
            scalars=1,
        )
        got = to_y(give, lambda b, step=step: b ^ (1 << step))
    down_grad = (keep.astype(F32) + got.astype(F32)).astype(B16)
    return mixed, token_grad, down_grad.T[None]


def solution(mesh):
    dp, owners, tensor = (mesh.shape[a] for a in ("dp", "expert", "tensor"))
    mesh = jax.sharding.Mesh(
        mesh.devices.reshape(dp // NX, NX, owners, tensor), ("y", "x", "expert", "tensor")
    )
    blocks = ("y", "x", "expert")
    placed = (
        P(blocks, "tensor"),
        P(blocks, None),
        P(blocks, None),
        P("expert", None, "tensor"),
        P("expert", None, "tensor"),
        P("expert", "tensor", None),
        P(blocks, "tensor"),
    )

    return jax.shard_map(
        per_device,
        mesh=mesh,
        in_specs=placed,
        out_specs=(P(blocks, "tensor"), P(blocks, "tensor"), P("expert", "tensor", ("y", "x"))),
        check_vma=False,
    )
```

```python
import functools
import math

import jax
import jax.numpy as jnp
from jax import lax
from jax.experimental import pallas as pl
from jax.experimental.pallas import tpu as pltpu
from jax.sharding import PartitionSpec as P

EXPERTS = 128
NX = 4
B16 = jnp.bfloat16
F32 = jnp.float32
ROWS0 = (((0,), (0,)), ((), ()))
COLS1 = (((1,), (1,)), ((), ()))


def dot(a, b, dims=None):
    if dims is None:
        dims = (((1,), (0,)), ((), ()))
    return lax.dot_general(a, b, dims, preferred_element_type=F32)


def hbm(v):
    return pltpu.with_memory_space_constraint(v, pltpu.HBM)


def fused(kernel, outs, *args, scalars=0, flops=0, mib=8):
    specs = [pl.BlockSpec(memory_space=pltpu.SMEM)] * scalars
    specs += [pl.BlockSpec(memory_space=pltpu.VMEM)] * (len(args) - scalars)
    nbytes = sum(math.prod(a.shape) * a.dtype.itemsize for a in list(args) + list(outs))
    return pl.pallas_call(
        kernel,
        out_shape=outs,
        in_specs=specs,
        out_specs=[pl.BlockSpec(memory_space=pltpu.VMEM)] * len(outs),
        compiler_params=pltpu.CompilerParams(vmem_limit_bytes=mib << 20),
        cost_estimate=pl.CostEstimate(flops=flops, bytes_accessed=nbytes, transcendentals=0),
    )(*args)


def routing(ids_ref, w_ref, owners, cap):
    choose, toks = ids_ref.shape
    expert = lax.broadcasted_iota(jnp.int32, (owners, toks), 0)
    mask = jnp.zeros((owners, toks), F32)
    weight = jnp.zeros((owners, toks), F32)
    for k in range(choose):
        hit = ids_ref[k : k + 1, :] == expert
        mask = mask + jnp.where(hit, 1.0, 0.0)
        weight = weight + jnp.where(hit, w_ref[k : k + 1, :], 0.0)
    earlier = lax.broadcasted_iota(jnp.int32, (toks, toks), 0) < lax.broadcasted_iota(
        jnp.int32, (toks, toks), 1
    )
    rank = dot(mask.astype(B16), jnp.where(earlier, 1.0, 0.0).astype(B16))
    code = jnp.where(mask > 0.0, rank, -100.0)
    shape = (owners, 2 * cap, toks)
    code = jnp.broadcast_to(code[:, None, :], shape)
    weight = jnp.broadcast_to(weight[:, None, :], shape)
    row = lax.broadcasted_iota(jnp.int32, shape, 1).astype(F32)
    flat = (owners * 2 * cap, toks)
    left = jnp.where(code == row, 1.0, 0.0).reshape(flat)
    right = jnp.where(code == row - float(cap), 1.0, 0.0).reshape(flat)
    return left, right, weight.reshape(flat)


def dispatch_kernel(owners, cap, ids_ref, w_ref, tok_ref, cot_ref, out_ref):
    left, right, weight = routing(ids_ref, w_ref, owners, cap)
    scale = jnp.sum(right * weight, axis=1, keepdims=True)
    rows = dot(left.astype(B16), tok_ref[...]) + dot(right.astype(B16), cot_ref[...]) * scale
    out_ref[...] = rows.astype(B16)


def plan_kernel(owners, cap, ids_ref, w_ref, high_ref, low_ref, right_ref):
    left, right, weight = routing(ids_ref, w_ref, owners, cap)
    left = (left * weight).T
    high = left.astype(B16)
    high_ref[...] = high
    low_ref[...] = (left - high.astype(F32)).astype(B16)
    right_ref[...] = right.T.astype(B16)


def combine_kernel(high_ref, low_ref, right_ref, rows_ref, mixed_ref, grad_ref):
    rows = rows_ref[...]
    mixed_ref[...] = (dot(high_ref[...], rows) + dot(low_ref[...], rows)).astype(B16)
    grad_ref[...] = dot(right_ref[...], rows).astype(B16)


def pick(shape, axis, cap, shift):
    compact = lax.broadcasted_iota(jnp.int32, shape, axis).astype(F32)
    chunk = lax.broadcasted_iota(jnp.int32, shape, 1 - axis).astype(F32)
    block = jnp.floor((compact + 0.5) * (1.0 / cap))
    return jnp.where(chunk == compact + cap * block + shift, 1.0, 0.0).astype(B16)


def halves(side_ref, half):
    side = side_ref[0]
    here = pl.ds(pl.multiple_of(side * half, half), half)
    there = pl.ds(pl.multiple_of((1 - side) * half, half), half)
    return side, here, there


def forward_kernel(cap, side_ref, own_ref, oth_ref, wg_ref, wu_ref, gate_ref, up_ref, pack_ref):
    rows, half = own_ref.shape
    slots = rows // 2
    _, here, there = halves(side_ref, half)
    own, oth = own_ref[...], oth_ref[...]
    to_x = pick((slots, rows), 0, cap, 0)
    x_own, x_oth = dot(to_x, own).astype(B16), dot(to_x, oth).astype(B16)
    gate = dot(x_own, wg_ref[here, :]) + dot(x_oth, wg_ref[there, :])
    up = dot(x_own, wu_ref[here, :]) + dot(x_oth, wu_ref[there, :])
    hidden = (gate * (1.0 / (1.0 + jnp.exp(-gate))) * up).astype(B16)
    gate_ref[...] = gate
    up_ref[...] = up
    g = dot(pick((slots, rows), 0, cap, cap), own).astype(B16)
    wide = half // NX
    nyh = wide // 64
    for xd in range(NX):
        cols = [g[:, (y * NX + xd) * 64 : (y * NX + xd) * 64 + 64] for y in range(nyh)]
        pack_ref[xd, :, 0 : wide // 2] = jnp.concatenate(cols[0::2], axis=1)
        pack_ref[xd, :, wide // 2 : wide] = jnp.concatenate(cols[1::2], axis=1)
        pack_ref[xd, :, wide:] = hidden


def backward_kernel(
    cap, side_ref, own_ref, oth_ref, gate_ref, up_ref, wg_ref, wu_ref, wd_ref, keep_ref, give_ref
):
    rows, half = own_ref.shape
    slots = rows // 2
    _, here, there = halves(side_ref, half)
    to_g = pick((slots, rows), 0, cap, cap)
    g_own, g_oth = dot(to_g, own_ref[...]).astype(B16), dot(to_g, oth_ref[...]).astype(B16)
    gate, up = gate_ref[...], up_ref[...]
    sig = 1.0 / (1.0 + jnp.exp(-gate))
    act = gate * sig
    hidden = (act * up).astype(B16)
    hidden_grad = dot(g_own, wd_ref[:, here], COLS1) + dot(g_oth, wd_ref[:, there], COLS1)
    gate_term = (hidden_grad * up * sig * (1.0 + gate * (1.0 - sig))).astype(B16)
    up_term = (hidden_grad * act).astype(B16)
    from_x = pick((rows, slots), 1, cap, 0)
    from_g = pick((rows, slots), 1, cap, cap)
    for part, out in ((there, give_ref), (here, keep_ref)):
        out_rows = dot(hidden, wd_ref[:, part]).astype(B16)
        row_grad = dot(gate_term, wg_ref[part, :], COLS1) + dot(up_term, wu_ref[part, :], COLS1)
        out[...] = (dot(from_x, out_rows) + dot(from_g, row_grad.astype(B16))).astype(B16)


def down_kernel(bit_ref, packs_ref, cols_ref, keep_ref, give_ref):
    n = keep_ref.shape[0] // 2
    slots = packs_ref.shape[1]
    wide = cols_ref.shape[2]
    bit = bit_ref[0]
    for at, out in ((1 - bit, give_ref), (bit, keep_ref)):
        cols = pl.ds(pl.multiple_of(at * n, n), n)
        for h in range(2):
            total = None
            for k in range(NX):
                rows = cols_ref[k, h * slots : (h + 1) * slots, cols]
                part = dot(rows, packs_ref[k, :, wide:], ROWS0)
                total = part if total is None else total + part
            out[h * n : (h + 1) * n, :] = total.astype(B16)


def partner_row(bit_ref, pair_ref, at, n):
    start = (1 - bit_ref[0]) * (pair_ref.shape[0] // 2) + at
    return pair_ref[pl.ds(pl.multiple_of(start, n), n), :].astype(F32)


def halve_kernel(blocks, last_ref, bit_ref, mine_ref, pair_ref, keep_ref, give_ref):
    n = keep_ref.shape[0] // blocks
    bit = bit_ref[0]
    for side, out in ((1 - bit, give_ref), (bit, keep_ref)):
        for k in range(blocks):
            at = (2 * k + side) * n
            mine = mine_ref[pl.ds(pl.multiple_of(at, n), n), :].astype(F32)
            both = mine + partner_row(last_ref, pair_ref, at, n)
            out[k * n : (k + 1) * n, :] = both.astype(B16)


def finish_kernel(last_ref, mine_ref, pair_ref, out_ref):
    n = out_ref.shape[0]
    out_ref[...] = (mine_ref[...].astype(F32) + partner_row(last_ref, pair_ref, 0, n)).astype(B16)


def per_device(tokens, expert_ids, route_weight, gate_weight, up_weight, down_weight, cotangent):
    owners = lax.axis_size("expert")
    tok_rows, choose = expert_ids.shape
    cap = 3 * tok_rows * choose // (2 * EXPERTS)
    half = tokens.shape[1]
    slots = owners * cap
    ff = gate_weight.shape[2]
    bf = lambda *shape: jax.ShapeDtypeStruct(shape, B16)
    side = lax.axis_index("tensor").astype(jnp.int32).reshape(1)
    bits = [lax.axis_index(a).astype(jnp.int32).reshape(1) for a in ("y1", "y2", "y4")]
    ids_t, w_t = expert_ids.T, route_weight.T
    (send,) = fused(
        functools.partial(dispatch_kernel, owners, cap),
        [bf(2 * slots, half)],
        hbm(ids_t),
        hbm(w_t),
        hbm(tokens),
        hbm(cotangent),
        flops=4 * slots * tok_rows * half * 2,
    )
    high, low, right = fused(
        functools.partial(plan_kernel, owners, cap),
        [bf(tok_rows, 2 * slots)] * 3,
        hbm(ids_t),
        hbm(w_t),
        flops=tok_rows**3,
    )

    def trade(rows, axis, *shape):
        return lax.all_to_all(rows.reshape(shape), axis, split_axis=0, concat_axis=0, tiled=True)

    def swap(v):
        return lax.ppermute(v, "tensor", [(0, 1), (1, 0)])

    def pair(v, axis, dim=0):
        return lax.all_gather(v, axis, axis=dim, tiled=True)

    chunks = (owners, 2 * cap, half)
    own = trade(send, "expert", *chunks).reshape(2 * slots, half)
    oth = swap(own)
    gate, up, pack = fused(
        functools.partial(forward_kernel, cap),
        [pltpu.HBM((slots, ff), F32)] * 2
        + [pltpu.HBM((NX, slots, half // NX + ff), B16)],
        side,
        own,
        oth,
        gate_weight[0],
        hbm(up_weight[0]),
        scalars=1,
        flops=slots * half * 2 * ff * 4 + slots * 2 * slots * half * 8,
        mib=20,
    )
    packs = trade(pack, "x", *pack.shape)
    keep, give = fused(
        functools.partial(backward_kernel, cap),
        [bf(2 * slots, half)] * 2,
        side,
        own,
        oth,
        gate,
        up,
        hbm(gate_weight[0]),
        hbm(up_weight[0]),
        hbm(down_weight[0]),
        scalars=1,
        flops=slots * half * 2 * ff * 8 + slots * 2 * slots * half * 12,
        mib=24,
    )
    total = (keep.astype(F32) + swap(give).astype(F32)).astype(B16)
    back = trade(total, "expert", *chunks).reshape(2 * slots, half)
    mixed, token_grad = fused(
        combine_kernel,
        [bf(tok_rows, half)] * 2,
        high,
        low,
        right,
        back,
        flops=tok_rows * 2 * slots * half * 6,
    )
    keep, give = fused(
        down_kernel,
        [bf(half // 4, ff)] * 2,
        bits[0],
        packs,
        pair(packs[:, :, : half // NX], "tensor", 1),
        scalars=1,
        flops=half // 2 * ff * slots * 2 * NX,
    )
    for step, blocks in ((1, 2), (2, 1)):
        rows = keep.shape[0] // 2
        keep, give = fused(
            functools.partial(halve_kernel, blocks),
            [bf(rows, ff)] * 2,
            bits[step - 1],
            bits[step],
            keep,
            pair(give, ("y1", "y2")[step - 1]),
            scalars=2,
        )
    (down_grad,) = fused(
        finish_kernel, [bf(*keep.shape)], bits[2], keep, pair(give, "y4"), scalars=1
    )
    return mixed, token_grad, down_grad.T[None]


def solution(mesh):
    dp, owners, tensor = (mesh.shape[a] for a in ("dp", "expert", "tensor"))
    mesh = jax.sharding.Mesh(
        mesh.devices.reshape(2, 2, dp // (4 * NX), NX, owners, tensor),
        ("y4", "y2", "y1", "x", "expert", "tensor"),
    )
    ways = ("y4", "y2", "y1", "x")
    blocks = (*ways, "expert")
    placed = (
        P(blocks, "tensor"),
        P(blocks, None),
        P(blocks, None),
        P("expert", None, "tensor"),
        P("expert", None, "tensor"),
        P("expert", "tensor", None),
        P(blocks, "tensor"),
    )

    return jax.shard_map(
        per_device,
        mesh=mesh,
        in_specs=placed,
        out_specs=(P(blocks, "tensor"), P(blocks, "tensor"), P("expert", "tensor", ways)),
        check_vma=False,
    )
```

```python
import functools
import math

import jax
import jax.numpy as jnp
from jax import lax
from jax.experimental import pallas as pl
from jax.experimental.pallas import tpu as pltpu
from jax.sharding import PartitionSpec as P

EXPERTS = 128
NX = 4
B16 = jnp.bfloat16
F32 = jnp.float32
ROWS0 = (((0,), (0,)), ((), ()))
COLS1 = (((1,), (1,)), ((), ()))


def dot(a, b, dims=None):
    if dims is None:
        dims = (((1,), (0,)), ((), ()))
    return lax.dot_general(a, b, dims, preferred_element_type=F32)


def hbm(v):
    return pltpu.with_memory_space_constraint(v, pltpu.HBM)


def fused(kernel, outs, *args, scalars=0, flops=0, mib=8, far=(), scratch=()):
    specs = [
        pl.BlockSpec(
            memory_space=pltpu.SMEM if i < scalars else pltpu.HBM if i in far else pltpu.VMEM
        )
        for i in range(len(args))
    ]
    nbytes = sum(math.prod(a.shape) * a.dtype.itemsize for a in list(args) + list(outs))
    return pl.pallas_call(
        kernel,
        out_shape=outs,
        in_specs=specs,
        out_specs=[pl.BlockSpec(memory_space=pltpu.VMEM)] * len(outs),
        scratch_shapes=scratch,
        compiler_params=pltpu.CompilerParams(vmem_limit_bytes=mib << 20),
        cost_estimate=pl.CostEstimate(flops=flops, bytes_accessed=nbytes, transcendentals=0),
    )(*args)


def fetch(pairs, sems):
    copies = [pltpu.make_async_copy(a, b, sems.at[i]) for i, (a, b) in enumerate(pairs)]
    for c in copies:
        c.start()
    return copies


def landing(*shapes):
    return [pltpu.VMEM(v.shape, v.dtype) for v in shapes] + [
        pltpu.SemaphoreType.DMA((len(shapes),))
    ]


def routing(ids_ref, w_ref, owners, cap):
    choose, toks = ids_ref.shape
    expert = lax.broadcasted_iota(jnp.int32, (owners, toks), 0)
    mask = jnp.zeros((owners, toks), F32)
    weight = jnp.zeros((owners, toks), F32)
    for k in range(choose):
        hit = ids_ref[k : k + 1, :] == expert
        mask = mask + jnp.where(hit, 1.0, 0.0)
        weight = weight + jnp.where(hit, w_ref[k : k + 1, :], 0.0)
    earlier = lax.broadcasted_iota(jnp.int32, (toks, toks), 0) < lax.broadcasted_iota(
        jnp.int32, (toks, toks), 1
    )
    rank = dot(mask.astype(B16), jnp.where(earlier, 1.0, 0.0).astype(B16))
    code = jnp.where(mask > 0.0, rank, -100.0)
    shape = (owners, 2 * cap, toks)
    code = jnp.broadcast_to(code[:, None, :], shape)
    weight = jnp.broadcast_to(weight[:, None, :], shape)
    row = lax.broadcasted_iota(jnp.int32, shape, 1).astype(F32)
    flat = (owners * 2 * cap, toks)
    left = jnp.where(code == row, 1.0, 0.0).reshape(flat)
    right = jnp.where(code == row - float(cap), 1.0, 0.0).reshape(flat)
    return left, right, weight.reshape(flat)


def dispatch_kernel(owners, cap, *refs):
    sources, out_ref, landed, sems = refs[:4], refs[4], refs[5:9], refs[9]
    copies = fetch(list(zip(sources, landed, strict=True)), sems)
    ids_ref, w_ref, tok_ref, cot_ref = landed
    copies[0].wait()
    copies[1].wait()
    left, right, weight = routing(ids_ref, w_ref, owners, cap)
    scale = jnp.sum(right * weight, axis=1, keepdims=True)
    left, right = left.astype(B16), right.astype(B16)
    copies[2].wait()
    copies[3].wait()
    out_ref[...] = (dot(left, tok_ref[...]) + dot(right, cot_ref[...]) * scale).astype(B16)


def plan_kernel(owners, cap, ids_ref, w_ref, high_ref, low_ref, right_ref):
    left, right, weight = routing(ids_ref, w_ref, owners, cap)
    left = (left * weight).T
    high = left.astype(B16)
    high_ref[...] = high
    low_ref[...] = (left - high.astype(F32)).astype(B16)
    right_ref[...] = right.T.astype(B16)


def combine_kernel(high_ref, low_ref, right_ref, rows_ref, mixed_ref, grad_ref):
    rows = rows_ref[...]
    mixed_ref[...] = (dot(high_ref[...], rows) + dot(low_ref[...], rows)).astype(B16)
    grad_ref[...] = dot(right_ref[...], rows).astype(B16)


def pick(shape, axis, cap, shift):
    compact = lax.broadcasted_iota(jnp.int32, shape, axis).astype(F32)
    chunk = lax.broadcasted_iota(jnp.int32, shape, 1 - axis).astype(F32)
    block = jnp.floor((compact + 0.5) * (1.0 / cap))
    return jnp.where(chunk == compact + cap * block + shift, 1.0, 0.0).astype(B16)


def halves(side_ref, half):
    side = side_ref[0]
    here = pl.ds(pl.multiple_of(side * half, half), half)
    there = pl.ds(pl.multiple_of((1 - side) * half, half), half)
    return side, here, there


def own_kernel(cap, side_ref, own_ref, wg_far, wu_far, gate_ref, up_ref, cols_ref, wg, wu, sems):
    rows, half = own_ref.shape
    slots = rows // 2
    _, here, _ = halves(side_ref, half)
    copies = fetch([(wg_far.at[here], wg), (wu_far.at[here], wu)], sems)
    own = own_ref[...]
    x = dot(pick((slots, rows), 0, cap, 0), own).astype(B16)
    g = dot(pick((slots, rows), 0, cap, cap), own).astype(B16)
    wide = half // NX
    for xd in range(NX):
        cols = [g[:, (y * NX + xd) * 64 : (y * NX + xd) * 64 + 64] for y in range(wide // 64)]
        cols_ref[xd, :, 0 : wide // 2] = jnp.concatenate(cols[0::2], axis=1)
        cols_ref[xd, :, wide // 2 : wide] = jnp.concatenate(cols[1::2], axis=1)
    copies[0].wait()
    gate_ref[...] = dot(x, wg[...])
    copies[1].wait()
    up_ref[...] = dot(x, wu[...])


def rest_kernel(
    cap, side_ref, oth_ref, gate_in, up_in, cols_ref, wg_far, wu_far, gate_ref, up_ref, pack_ref, wg, wu, sems
):
    rows, half = oth_ref.shape
    slots = rows // 2
    _, _, there = halves(side_ref, half)
    copies = fetch([(wg_far.at[there], wg), (wu_far.at[there], wu)], sems)
    wide = cols_ref.shape[2]
    x = dot(pick((slots, rows), 0, cap, 0), oth_ref[...]).astype(B16)
    pack_ref[:, :, 0:wide] = cols_ref[...]
    copies[0].wait()
    gate = gate_in[...] + dot(x, wg[...])
    copies[1].wait()
    up = up_in[...] + dot(x, wu[...])
    hidden = (gate * (1.0 / (1.0 + jnp.exp(-gate))) * up).astype(B16)
    gate_ref[...] = gate
    up_ref[...] = up
    for xd in range(NX):
        pack_ref[xd, :, wide:] = hidden


def backward_kernel(
    cap, side_ref, own_ref, oth_ref, gate_ref, up_ref, wg_ref, wu_ref, wd_ref, keep_ref, give_ref
):
    rows, half = own_ref.shape
    slots = rows // 2
    _, here, there = halves(side_ref, half)
    to_g = pick((slots, rows), 0, cap, cap)
    g_own, g_oth = dot(to_g, own_ref[...]).astype(B16), dot(to_g, oth_ref[...]).astype(B16)
    gate, up = gate_ref[...], up_ref[...]
    sig = 1.0 / (1.0 + jnp.exp(-gate))
    act = gate * sig
    hidden = (act * up).astype(B16)
    hidden_grad = dot(g_own, wd_ref[:, here], COLS1) + dot(g_oth, wd_ref[:, there], COLS1)
    gate_term = (hidden_grad * up * sig * (1.0 + gate * (1.0 - sig))).astype(B16)
    up_term = (hidden_grad * act).astype(B16)
    from_x = pick((rows, slots), 1, cap, 0)
    from_g = pick((rows, slots), 1, cap, cap)
    for part, out in ((there, give_ref), (here, keep_ref)):
        out_rows = dot(hidden, wd_ref[:, part]).astype(B16)
        row_grad = dot(gate_term, wg_ref[part, :], COLS1) + dot(up_term, wu_ref[part, :], COLS1)
        out[...] = (dot(from_x, out_rows) + dot(from_g, row_grad.astype(B16))).astype(B16)


def down_kernel(bit_ref, packs_ref, cols_ref, keep_ref, give_ref):
    n = keep_ref.shape[0] // 2
    slots = packs_ref.shape[1]
    wide = cols_ref.shape[2]
    bit = bit_ref[0]
    for at, out in ((1 - bit, give_ref), (bit, keep_ref)):
        cols = pl.ds(pl.multiple_of(at * n, n), n)
        for h in range(2):
            total = None
            for k in range(NX):
                rows = cols_ref[k, h * slots : (h + 1) * slots, cols]
                part = dot(rows, packs_ref[k, :, wide:], ROWS0)
                total = part if total is None else total + part
            out[h * n : (h + 1) * n, :] = total.astype(B16)


def partner_row(bit_ref, pair_ref, at, n):
    start = (1 - bit_ref[0]) * (pair_ref.shape[0] // 2) + at
    return pair_ref[pl.ds(pl.multiple_of(start, n), n), :].astype(F32)


def halve_kernel(blocks, last_ref, bit_ref, mine_ref, pair_ref, keep_ref, give_ref):
    n = keep_ref.shape[0] // blocks
    bit = bit_ref[0]
    for side, out in ((1 - bit, give_ref), (bit, keep_ref)):
        for k in range(blocks):
            at = (2 * k + side) * n
            mine = mine_ref[pl.ds(pl.multiple_of(at, n), n), :].astype(F32)
            both = mine + partner_row(last_ref, pair_ref, at, n)
            out[k * n : (k + 1) * n, :] = both.astype(B16)


def finish_kernel(last_ref, mine_ref, pair_ref, out_ref):
    n = out_ref.shape[0]
    out_ref[...] = (mine_ref[...].astype(F32) + partner_row(last_ref, pair_ref, 0, n)).astype(B16)


def per_device(tokens, expert_ids, route_weight, gate_weight, up_weight, down_weight, cotangent):
    owners = lax.axis_size("expert")
    tok_rows, choose = expert_ids.shape
    cap = 3 * tok_rows * choose // (2 * EXPERTS)
    half = tokens.shape[1]
    slots = owners * cap
    ff = gate_weight.shape[2]
    bf = lambda *shape: jax.ShapeDtypeStruct(shape, B16)
    side = lax.axis_index("tensor").astype(jnp.int32).reshape(1)
    bits = [lax.axis_index(a).astype(jnp.int32).reshape(1) for a in ("y1", "y2", "y4")]
    ids_t, w_t = expert_ids.T, route_weight.T
    (send,) = fused(
        functools.partial(dispatch_kernel, owners, cap),
        [bf(2 * slots, half)],
        hbm(ids_t),
        hbm(w_t),
        hbm(tokens),
        hbm(cotangent),
        flops=4 * slots * tok_rows * half * 2,
        far=range(4),
        scratch=landing(ids_t, w_t, tokens, cotangent),
    )
    high, low, right = fused(
        functools.partial(plan_kernel, owners, cap),
        [bf(tok_rows, 2 * slots)] * 3,
        hbm(ids_t),
        hbm(w_t),
        flops=tok_rows**3,
    )

    def trade(rows, axis, *shape):
        return lax.all_to_all(rows.reshape(shape), axis, split_axis=0, concat_axis=0, tiled=True)

    def swap(v):
        return lax.ppermute(v, "tensor", [(0, 1), (1, 0)])

    def pair(v, axis, dim=0):
        return lax.all_gather(v, axis, axis=dim, tiled=True)

    chunks = (owners, 2 * cap, half)
    own = trade(send, "expert", *chunks).reshape(2 * slots, half)
    oth = swap(own)
    floats = jax.ShapeDtypeStruct((slots, ff), F32)
    halfway = landing(bf(half, ff), bf(half, ff))
    gate, up, cols = fused(
        functools.partial(own_kernel, cap),
        [floats, floats, bf(NX, slots, half // NX)],
        side,
        own,
        hbm(gate_weight[0]),
        hbm(up_weight[0]),
        scalars=1,
        flops=slots * half * 2 * ff * 2 + slots * 2 * slots * half * 4,
        mib=12,
        far=(2, 3),
        scratch=halfway,
    )
    gate, up, pack = fused(
        functools.partial(rest_kernel, cap),
        [pltpu.HBM((slots, ff), F32)] * 2 + [pltpu.HBM((NX, slots, half // NX + ff), B16)],
        side,
        oth,
        gate,
        up,
        cols,
        hbm(gate_weight[0]),
        hbm(up_weight[0]),
        scalars=1,
        flops=slots * half * 2 * ff * 2 + slots * 2 * slots * half * 2,
        mib=12,
        far=(5, 6),
        scratch=halfway,
    )
    packs = trade(pack, "x", *pack.shape)
    keep, give = fused(
        functools.partial(backward_kernel, cap),
        [bf(2 * slots, half)] * 2,
        side,
        own,
        oth,
        gate,
        up,
        hbm(gate_weight[0]),
        hbm(up_weight[0]),
        hbm(down_weight[0]),
        scalars=1,
        flops=slots * half * 2 * ff * 8 + slots * 2 * slots * half * 12,
        mib=24,
    )
    total = (keep.astype(F32) + swap(give).astype(F32)).astype(B16)
    back = trade(total, "expert", *chunks).reshape(2 * slots, half)
    mixed, token_grad = fused(
        combine_kernel,
        [bf(tok_rows, half)] * 2,
        high,
        low,
        right,
        back,
        flops=tok_rows * 2 * slots * half * 6,
    )
    keep, give = fused(
        down_kernel,
        [bf(half // 4, ff)] * 2,
        bits[0],
        packs,
        pair(packs[:, :, : half // NX], "tensor", 1),
        scalars=1,
        flops=half // 2 * ff * slots * 2 * NX,
    )
    for step, blocks in ((1, 2), (2, 1)):
        rows = keep.shape[0] // 2
        keep, give = fused(
            functools.partial(halve_kernel, blocks),
            [bf(rows, ff)] * 2,
            bits[step - 1],
            bits[step],
            keep,
            pair(give, ("y1", "y2")[step - 1]),
            scalars=2,
        )
    (down_grad,) = fused(
        finish_kernel, [bf(*keep.shape)], bits[2], keep, pair(give, "y4"), scalars=1
    )
    return mixed, token_grad, down_grad.T[None]


def solution(mesh):
    dp, owners, tensor = (mesh.shape[a] for a in ("dp", "expert", "tensor"))
    mesh = jax.sharding.Mesh(
        mesh.devices.reshape(2, 2, dp // (4 * NX), NX, owners, tensor),
        ("y4", "y2", "y1", "x", "expert", "tensor"),
    )
    ways = ("y4", "y2", "y1", "x")
    blocks = (*ways, "expert")
    placed = (
        P(blocks, "tensor"),
        P(blocks, None),
        P(blocks, None),
        P("expert", None, "tensor"),
        P("expert", None, "tensor"),
        P("expert", "tensor", None),
        P(blocks, "tensor"),
    )

    return jax.shard_map(
        per_device,
        mesh=mesh,
        in_specs=placed,
        out_specs=(P(blocks, "tensor"), P(blocks, "tensor"), P("expert", "tensor", ways)),
        check_vma=False,
    )
```

```python
import functools
import math

import jax
import jax.numpy as jnp
from jax import lax
from jax.experimental import pallas as pl
from jax.experimental.pallas import tpu as pltpu
from jax.sharding import PartitionSpec as P

EXPERTS = 128
NX = 4
B16 = jnp.bfloat16
F32 = jnp.float32
ROWS0 = (((0,), (0,)), ((), ()))
COLS1 = (((1,), (1,)), ((), ()))


def dot(a, b, dims=None):
    if dims is None:
        dims = (((1,), (0,)), ((), ()))
    return lax.dot_general(a, b, dims, preferred_element_type=F32)


def hbm(v):
    return pltpu.with_memory_space_constraint(v, pltpu.HBM)


def fused(kernel, outs, *args, scalars=0, flops=0, mib=8, far=(), scratch=()):
    specs = [
        pl.BlockSpec(
            memory_space=pltpu.SMEM if i < scalars else pltpu.HBM if i in far else pltpu.VMEM
        )
        for i in range(len(args))
    ]
    nbytes = sum(math.prod(a.shape) * a.dtype.itemsize for a in list(args) + list(outs))
    return pl.pallas_call(
        kernel,
        out_shape=outs,
        in_specs=specs,
        out_specs=[pl.BlockSpec(memory_space=pltpu.VMEM)] * len(outs),
        scratch_shapes=scratch,
        compiler_params=pltpu.CompilerParams(vmem_limit_bytes=mib << 20),
        cost_estimate=pl.CostEstimate(flops=flops, bytes_accessed=nbytes, transcendentals=0),
    )(*args)


def fetch(pairs, sems):
    copies = [pltpu.make_async_copy(a, b, sems.at[i]) for i, (a, b) in enumerate(pairs)]
    for c in copies:
        c.start()
    return copies


def landing(*shapes):
    return [pltpu.VMEM(v.shape, v.dtype) for v in shapes] + [
        pltpu.SemaphoreType.DMA((len(shapes),))
    ]


def routing(ids_ref, w_ref, owners, cap):
    choose, toks = ids_ref.shape
    expert = lax.broadcasted_iota(jnp.int32, (owners, toks), 0)
    mask = jnp.zeros((owners, toks), F32)
    weight = jnp.zeros((owners, toks), F32)
    for k in range(choose):
        hit = ids_ref[k : k + 1, :] == expert
        mask = mask + jnp.where(hit, 1.0, 0.0)
        weight = weight + jnp.where(hit, w_ref[k : k + 1, :], 0.0)
    earlier = lax.broadcasted_iota(jnp.int32, (toks, toks), 0) < lax.broadcasted_iota(
        jnp.int32, (toks, toks), 1
    )
    rank = dot(mask.astype(B16), jnp.where(earlier, 1.0, 0.0).astype(B16))
    code = jnp.where(mask > 0.0, rank, -100.0)
    shape = (owners, 2 * cap, toks)
    code = jnp.broadcast_to(code[:, None, :], shape)
    weight = jnp.broadcast_to(weight[:, None, :], shape)
    row = lax.broadcasted_iota(jnp.int32, shape, 1).astype(F32)
    flat = (owners * 2 * cap, toks)
    left = jnp.where(code == row, 1.0, 0.0).reshape(flat)
    right = jnp.where(code == row - float(cap), 1.0, 0.0).reshape(flat)
    return left, right, weight.reshape(flat)


def dispatch_kernel(owners, cap, *refs):
    sources, out_ref, landed, sems = refs[:4], refs[4], refs[5:9], refs[9]
    copies = fetch(list(zip(sources, landed, strict=True)), sems)
    ids_ref, w_ref, tok_ref, cot_ref = landed
    copies[0].wait()
    copies[1].wait()
    left, right, weight = routing(ids_ref, w_ref, owners, cap)
    scale = jnp.sum(right * weight, axis=1, keepdims=True)
    left, right = left.astype(B16), right.astype(B16)
    copies[2].wait()
    copies[3].wait()
    out_ref[...] = (dot(left, tok_ref[...]) + dot(right, cot_ref[...]) * scale).astype(B16)


def plan_kernel(owners, cap, ids_ref, w_ref, high_ref, low_ref, right_ref):
    left, right, weight = routing(ids_ref, w_ref, owners, cap)
    left = (left * weight).T
    high = left.astype(B16)
    high_ref[...] = high
    low_ref[...] = (left - high.astype(F32)).astype(B16)
    right_ref[...] = right.T.astype(B16)


def combine_kernel(
    bit_ref, high_ref, low_ref, right_ref, rows_ref, mine_ref, pair_ref, mixed_ref, grad_ref, down_ref
):
    n = mine_ref.shape[1]
    for h in range(2):
        both = mine_ref[h].astype(F32) + partner(bit_ref, pair_ref, h, 0, n)
        down_ref[h * n : (h + 1) * n, :] = both.astype(B16)
    rows = rows_ref[...]
    mixed_ref[...] = (dot(high_ref[...], rows) + dot(low_ref[...], rows)).astype(B16)
    grad_ref[...] = dot(right_ref[...], rows).astype(B16)


def pick(shape, axis, cap, shift):
    compact = lax.broadcasted_iota(jnp.int32, shape, axis).astype(F32)
    chunk = lax.broadcasted_iota(jnp.int32, shape, 1 - axis).astype(F32)
    block = jnp.floor((compact + 0.5) * (1.0 / cap))
    return jnp.where(chunk == compact + cap * block + shift, 1.0, 0.0).astype(B16)


def halves(side_ref, half):
    side = side_ref[0]
    here = pl.ds(pl.multiple_of(side * half, half), half)
    there = pl.ds(pl.multiple_of((1 - side) * half, half), half)
    return side, here, there


def own_kernel(cap, side_ref, own_ref, wg_ref, wu_far, gate_ref, up_ref, cols_ref, wu, sems):
    rows, half = own_ref.shape
    slots = rows // 2
    _, here, _ = halves(side_ref, half)
    copies = fetch([(wu_far.at[here], wu)], sems)
    own = own_ref[...]
    x = dot(pick((slots, rows), 0, cap, 0), own).astype(B16)
    g = dot(pick((slots, rows), 0, cap, cap), own).astype(B16)
    wide = half // NX
    for xd in range(NX):
        cols = [g[:, (y * NX + xd) * 64 : (y * NX + xd) * 64 + 64] for y in range(wide // 64)]
        cols_ref[xd, :, 0 : wide // 2] = jnp.concatenate(cols[0::2], axis=1)
        cols_ref[xd, :, wide // 2 : wide] = jnp.concatenate(cols[1::2], axis=1)
    gate_ref[...] = dot(x, wg_ref[here, :])
    copies[0].wait()
    up_ref[...] = dot(x, wu[...])


def rest_kernel(
    cap, side_ref, oth_ref, gate_in, up_in, cols_ref, wg_ref, wu_far, gate_ref, up_ref, pack_ref, wu, sems
):
    rows, half = oth_ref.shape
    slots = rows // 2
    _, _, there = halves(side_ref, half)
    copies = fetch([(wu_far.at[there], wu)], sems)
    wide = cols_ref.shape[2]
    x = dot(pick((slots, rows), 0, cap, 0), oth_ref[...]).astype(B16)
    pack_ref[:, :, 0:wide] = cols_ref[...]
    gate = gate_in[...] + dot(x, wg_ref[there, :])
    copies[0].wait()
    up = up_in[...] + dot(x, wu[...])
    hidden = (gate * (1.0 / (1.0 + jnp.exp(-gate))) * up).astype(B16)
    gate_ref[...] = gate
    up_ref[...] = up
    for xd in range(NX):
        pack_ref[xd, :, wide:] = hidden


def backward_kernel(
    cap, side_ref, own_ref, oth_ref, gate_ref, up_ref, wg_ref, wu_ref, wd_ref, keep_ref, give_ref
):
    rows, half = own_ref.shape
    slots = rows // 2
    _, here, there = halves(side_ref, half)
    to_g = pick((slots, rows), 0, cap, cap)
    g_own, g_oth = dot(to_g, own_ref[...]).astype(B16), dot(to_g, oth_ref[...]).astype(B16)
    gate, up = gate_ref[...], up_ref[...]
    sig = 1.0 / (1.0 + jnp.exp(-gate))
    act = gate * sig
    hidden = (act * up).astype(B16)
    hidden_grad = dot(g_own, wd_ref[:, here], COLS1) + dot(g_oth, wd_ref[:, there], COLS1)
    gate_term = (hidden_grad * up * sig * (1.0 + gate * (1.0 - sig))).astype(B16)
    up_term = (hidden_grad * act).astype(B16)
    from_x = pick((rows, slots), 1, cap, 0)
    from_g = pick((rows, slots), 1, cap, cap)
    for part, out in ((there, give_ref), (here, keep_ref)):
        out_rows = dot(hidden, wd_ref[:, part]).astype(B16)
        row_grad = dot(gate_term, wg_ref[part, :], COLS1) + dot(up_term, wu_ref[part, :], COLS1)
        out[...] = (dot(from_x, out_rows) + dot(from_g, row_grad.astype(B16))).astype(B16)


def down_kernel(bit_ref, packs_ref, cols_ref, keep_ref, give_ref):
    n = keep_ref.shape[1]
    slots = packs_ref.shape[1]
    wide = cols_ref.shape[2]
    bit = bit_ref[0]
    for at, out in ((1 - bit, give_ref), (bit, keep_ref)):
        cols = pl.ds(pl.multiple_of(at * n, n), n)
        for h in range(2):
            total = None
            for k in range(NX):
                rows = cols_ref[k, h * slots : (h + 1) * slots, cols]
                part = dot(rows, packs_ref[k, :, wide:], ROWS0)
                total = part if total is None else total + part
            out[h] = total.astype(B16)


def partner(bit_ref, pair_ref, h, at, n):
    start = (1 - bit_ref[0]) * (pair_ref.shape[1] // 2) + at
    return pair_ref[h, pl.ds(pl.multiple_of(start, n), n), :].astype(F32)


def halve_rows_kernel(last_ref, bit_ref, mine_ref, pair_ref, keep_ref, give_ref):
    n = keep_ref.shape[1]
    bit = bit_ref[0]
    for side, out in ((1 - bit, give_ref), (bit, keep_ref)):
        for h in range(2):
            mine = mine_ref[h, pl.ds(pl.multiple_of(side * n, n), n), :].astype(F32)
            out[h] = (mine + partner(last_ref, pair_ref, h, side * n, n)).astype(B16)


def halve_sides_kernel(last_ref, bit_ref, mine_ref, pair_ref, keep_ref, give_ref):
    n = keep_ref.shape[1]
    bit = bit_ref[0]
    for side, out in ((1 - bit, give_ref), (bit, keep_ref)):
        both = mine_ref[side].astype(F32) + partner(last_ref, pair_ref, side, 0, 2 * n)
        both = both.astype(B16)
        out[0] = both[0:n]
        out[1] = both[n : 2 * n]


def per_device(tokens, expert_ids, route_weight, gate_weight, up_weight, down_weight, cotangent):
    owners = lax.axis_size("expert")
    tok_rows, choose = expert_ids.shape
    cap = 3 * tok_rows * choose // (2 * EXPERTS)
    half = tokens.shape[1]
    slots = owners * cap
    ff = gate_weight.shape[2]
    bf = lambda *shape: jax.ShapeDtypeStruct(shape, B16)
    side = lax.axis_index("tensor").astype(jnp.int32).reshape(1)
    bits = [lax.axis_index(a).astype(jnp.int32).reshape(1) for a in ("y1", "y2", "y4")]
    ids_t, w_t = expert_ids.T, route_weight.T
    (send,) = fused(
        functools.partial(dispatch_kernel, owners, cap),
        [bf(2 * slots, half)],
        hbm(ids_t),
        hbm(w_t),
        hbm(tokens),
        hbm(cotangent),
        flops=4 * slots * tok_rows * half * 2,
        far=range(4),
        scratch=landing(ids_t, w_t, tokens, cotangent),
    )
    high, low, right = fused(
        functools.partial(plan_kernel, owners, cap),
        [bf(tok_rows, 2 * slots)] * 3,
        hbm(ids_t),
        hbm(w_t),
        flops=tok_rows**3,
    )

    def trade(rows, axis, *shape):
        return lax.all_to_all(rows.reshape(shape), axis, split_axis=0, concat_axis=0, tiled=True)

    def swap(v):
        return lax.ppermute(v, "tensor", [(0, 1), (1, 0)])

    def pair(v, axis):
        return lax.all_gather(v, axis, axis=1, tiled=True)

    chunks = (owners, 2 * cap, half)
    own = trade(send, "expert", *chunks).reshape(2 * slots, half)
    oth = swap(own)
    floats = jax.ShapeDtypeStruct((slots, ff), F32)
    halfway = landing(bf(half, ff))
    gate, up, cols = fused(
        functools.partial(own_kernel, cap),
        [floats, floats, bf(NX, slots, half // NX)],
        side,
        own,
        gate_weight[0],
        hbm(up_weight[0]),
        scalars=1,
        flops=slots * half * 2 * ff * 2 + slots * 2 * slots * half * 4,
        mib=12,
        far=(3,),
        scratch=halfway,
    )
    gate, up, pack = fused(
        functools.partial(rest_kernel, cap),
        [pltpu.HBM((slots, ff), F32)] * 2 + [pltpu.HBM((NX, slots, half // NX + ff), B16)],
        side,
        oth,
        gate,
        up,
        cols,
        gate_weight[0],
        hbm(up_weight[0]),
        scalars=1,
        flops=slots * half * 2 * ff * 2 + slots * 2 * slots * half * 2,
        mib=12,
        far=(6,),
        scratch=halfway,
    )
    packs = trade(pack, "x", *pack.shape)
    keep, give = fused(
        functools.partial(backward_kernel, cap),
        [bf(2 * slots, half)] * 2,
        side,
        own,
        oth,
        gate,
        up,
        hbm(gate_weight[0]),
        hbm(up_weight[0]),
        hbm(down_weight[0]),
        scalars=1,
        flops=slots * half * 2 * ff * 8 + slots * 2 * slots * half * 12,
        mib=24,
    )
    total = (keep.astype(F32) + swap(give).astype(F32)).astype(B16)
    back = trade(total, "expert", *chunks).reshape(2 * slots, half)
    keep, give = fused(
        down_kernel,
        [bf(2, half // 8, ff)] * 2,
        bits[0],
        packs,
        pair(packs[:, :, : half // NX], "tensor"),
        scalars=1,
        flops=half // 2 * ff * slots * 2 * NX,
    )
    for step, kernel in ((1, halve_rows_kernel), (2, halve_sides_kernel)):
        keep, give = fused(
            kernel,
            [bf(2, keep.shape[1] // 2, ff)] * 2,
            bits[step - 1],
            bits[step],
            keep,
            pair(give, ("y1", "y2")[step - 1]),
            scalars=2,
        )
    mixed, token_grad, down_grad = fused(
        combine_kernel,
        [bf(tok_rows, half)] * 2 + [bf(half // 16, ff)],
        bits[2],
        high,
        low,
        right,
        back,
        keep,
        pair(give, "y4"),
        scalars=1,
        flops=tok_rows * 2 * slots * half * 6,
    )
    return mixed, token_grad, down_grad.T[None]


def solution(mesh):
    dp, owners, tensor = (mesh.shape[a] for a in ("dp", "expert", "tensor"))
    mesh = jax.sharding.Mesh(
        mesh.devices.reshape(2, 2, dp // (4 * NX), NX, owners, tensor),
        ("y4", "y2", "y1", "x", "expert", "tensor"),
    )
    ways = ("y4", "y2", "y1", "x")
    blocks = (*ways, "expert")
    placed = (
        P(blocks, "tensor"),
        P(blocks, None),
        P(blocks, None),
        P("expert", None, "tensor"),
        P("expert", None, "tensor"),
        P("expert", "tensor", None),
        P(blocks, "tensor"),
    )

    return jax.shard_map(
        per_device,
        mesh=mesh,
        in_specs=placed,
        out_specs=(P(blocks, "tensor"), P(blocks, "tensor"), P("expert", "tensor", ways)),
        check_vma=False,
    )
```

```python
import functools
import math

import jax
import jax.numpy as jnp
from jax import lax
from jax.experimental import pallas as pl
from jax.experimental.pallas import tpu as pltpu
from jax.sharding import PartitionSpec as P

EXPERTS = 128
NX = 4
B16 = jnp.bfloat16
F32 = jnp.float32
ROWS0 = (((0,), (0,)), ((), ()))
COLS1 = (((1,), (1,)), ((), ()))


def dot(a, b, dims=None):
    if dims is None:
        dims = (((1,), (0,)), ((), ()))
    return lax.dot_general(a, b, dims, preferred_element_type=F32)


def hbm(v):
    return pltpu.with_memory_space_constraint(v, pltpu.HBM)


def fused(kernel, outs, *args, scalars=0, flops=0, mib=8, far=(), scratch=(), alias=None):
    specs = [
        pl.BlockSpec(
            memory_space=pltpu.SMEM if i < scalars else pltpu.HBM if i in far else pltpu.VMEM
        )
        for i in range(len(args))
    ]
    nbytes = sum(math.prod(a.shape) * a.dtype.itemsize for a in list(args) + list(outs))
    return pl.pallas_call(
        kernel,
        out_shape=outs,
        in_specs=specs,
        out_specs=[pl.BlockSpec(memory_space=pltpu.VMEM)] * len(outs),
        scratch_shapes=scratch,
        input_output_aliases=alias or {},
        compiler_params=pltpu.CompilerParams(vmem_limit_bytes=mib << 20),
        cost_estimate=pl.CostEstimate(flops=flops, bytes_accessed=nbytes, transcendentals=0),
    )(*args)


def fetch(pairs, sems):
    copies = [pltpu.make_async_copy(a, b, sems.at[i]) for i, (a, b) in enumerate(pairs)]
    for c in copies:
        c.start()
    return copies


def landing(*shapes):
    return [pltpu.VMEM(v.shape, v.dtype) for v in shapes] + [
        pltpu.SemaphoreType.DMA((len(shapes),))
    ]


def routing(ids_ref, w_ref, owners, cap):
    choose, toks = ids_ref.shape
    expert = lax.broadcasted_iota(jnp.int32, (owners, toks), 0)
    mask = jnp.zeros((owners, toks), F32)
    weight = jnp.zeros((owners, toks), F32)
    for k in range(choose):
        hit = ids_ref[k : k + 1, :] == expert
        mask = mask + jnp.where(hit, 1.0, 0.0)
        weight = weight + jnp.where(hit, w_ref[k : k + 1, :], 0.0)
    earlier = lax.broadcasted_iota(jnp.int32, (toks, toks), 0) < lax.broadcasted_iota(
        jnp.int32, (toks, toks), 1
    )
    rank = dot(mask.astype(B16), jnp.where(earlier, 1.0, 0.0).astype(B16))
    code = jnp.where(mask > 0.0, rank, -100.0)
    shape = (owners, 2 * cap, toks)
    code = jnp.broadcast_to(code[:, None, :], shape)
    weight = jnp.broadcast_to(weight[:, None, :], shape)
    row = lax.broadcasted_iota(jnp.int32, shape, 1).astype(F32)
    flat = (owners * 2 * cap, toks)
    left = jnp.where(code == row, 1.0, 0.0).reshape(flat)
    right = jnp.where(code == row - float(cap), 1.0, 0.0).reshape(flat)
    return left, right, weight.reshape(flat)


def dispatch_kernel(owners, cap, *refs):
    sources, out_ref, landed, sems = refs[:4], refs[4], refs[5:9], refs[9]
    copies = fetch(list(zip(sources, landed, strict=True)), sems)
    ids_ref, w_ref, tok_ref, cot_ref = landed
    copies[0].wait()
    copies[1].wait()
    left, right, weight = routing(ids_ref, w_ref, owners, cap)
    scale = jnp.sum(right * weight, axis=1, keepdims=True)
    left, right = left.astype(B16), right.astype(B16)
    copies[2].wait()
    copies[3].wait()
    out_ref[...] = (dot(left, tok_ref[...]) + dot(right, cot_ref[...]) * scale).astype(B16)


def plan_kernel(owners, cap, ids_ref, w_ref, high_ref, low_ref, right_ref):
    left, right, weight = routing(ids_ref, w_ref, owners, cap)
    left = (left * weight).T
    high = left.astype(B16)
    high_ref[...] = high
    low_ref[...] = (left - high.astype(F32)).astype(B16)
    right_ref[...] = right.T.astype(B16)


def combine_kernel(
    bit_ref, high_ref, low_ref, right_ref, rows_ref, mine_ref, pair_ref, mixed_ref, grad_ref, down_ref
):
    n = mine_ref.shape[1]
    for h in range(2):
        both = mine_ref[h].astype(F32) + partner(bit_ref, pair_ref, h, 0, n)
        down_ref[h * n : (h + 1) * n, :] = both.astype(B16)
    rows = rows_ref[...]
    mixed_ref[...] = (dot(high_ref[...], rows) + dot(low_ref[...], rows)).astype(B16)
    grad_ref[...] = dot(right_ref[...], rows).astype(B16)


def pick(shape, axis, cap, shift):
    compact = lax.broadcasted_iota(jnp.int32, shape, axis).astype(F32)
    chunk = lax.broadcasted_iota(jnp.int32, shape, 1 - axis).astype(F32)
    block = jnp.floor((compact + 0.5) * (1.0 / cap))
    return jnp.where(chunk == compact + cap * block + shift, 1.0, 0.0).astype(B16)


def halves(side_ref, half):
    side = side_ref[0]
    here = pl.ds(pl.multiple_of(side * half, half), half)
    there = pl.ds(pl.multiple_of((1 - side) * half, half), half)
    return side, here, there


def own_kernel(cap, side_ref, own_ref, wg_ref, wu_far, gate_ref, up_ref, cols_ref, wu, sems):
    rows, half = own_ref.shape
    slots = rows // 2
    _, here, _ = halves(side_ref, half)
    copies = fetch([(wu_far.at[here], wu)], sems)
    own = own_ref[...]
    x = dot(pick((slots, rows), 0, cap, 0), own).astype(B16)
    g = dot(pick((slots, rows), 0, cap, cap), own).astype(B16)
    wide = half // NX
    for xd in range(NX):
        cols = [g[:, (y * NX + xd) * 64 : (y * NX + xd) * 64 + 64] for y in range(wide // 64)]
        cols_ref[xd, :, 0 : wide // 2] = jnp.concatenate(cols[0::2], axis=1)
        cols_ref[xd, :, wide // 2 : wide] = jnp.concatenate(cols[1::2], axis=1)
    gate_ref[...] = dot(x, wg_ref[here, :])
    copies[0].wait()
    up_ref[...] = dot(x, wu[...])


def rest_kernel(
    cap, side_ref, oth_ref, gate_in, up_in, cols_ref, wg_ref, wu_far, gate_ref, up_ref, pack_ref, wu, sems
):
    rows, half = oth_ref.shape
    slots = rows // 2
    _, _, there = halves(side_ref, half)
    copies = fetch([(wu_far.at[there], wu)], sems)
    wide = cols_ref.shape[2]
    x = dot(pick((slots, rows), 0, cap, 0), oth_ref[...]).astype(B16)
    pack_ref[:, :, 0:wide] = cols_ref[...]
    gate = gate_in[...] + dot(x, wg_ref[there, :])
    copies[0].wait()
    up = up_in[...] + dot(x, wu[...])
    hidden = (gate * (1.0 / (1.0 + jnp.exp(-gate))) * up).astype(B16)
    gate_ref[...] = gate
    up_ref[...] = up
    for xd in range(NX):
        pack_ref[xd, :, wide:] = hidden


def results(cap, hidden, gate_term, up_term, wd, wg, wu):
    slots = hidden.shape[0]
    out_rows = dot(hidden, wd[...]).astype(B16)
    row_grad = (dot(gate_term, wg[...], COLS1) + dot(up_term, wu[...], COLS1)).astype(B16)
    from_x = pick((2 * slots, slots), 1, cap, 0)
    from_g = pick((2 * slots, slots), 1, cap, cap)
    return (dot(from_x, out_rows) + dot(from_g, row_grad)).astype(B16)


def give_kernel(
    cap, side_ref, own_ref, oth_ref, gate_ref, up_ref, wg_far, wu_far, wd_far,
    give_ref, hidden_ref, gate_term_ref, up_term_ref, wd_own, wd_oth, wg, wu, sems,
):
    rows, half = own_ref.shape
    slots = rows // 2
    _, here, there = halves(side_ref, half)
    copies = fetch(
        [
            (wd_far.at[:, here], wd_own),
            (wd_far.at[:, there], wd_oth),
            (wg_far.at[there], wg),
            (wu_far.at[there], wu),
        ],
        sems,
    )
    to_g = pick((slots, rows), 0, cap, cap)
    g_own, g_oth = dot(to_g, own_ref[...]).astype(B16), dot(to_g, oth_ref[...]).astype(B16)
    gate, up = gate_ref[...], up_ref[...]
    sig = 1.0 / (1.0 + jnp.exp(-gate))
    act = gate * sig
    hidden = (act * up).astype(B16)
    copies[0].wait()
    copies[1].wait()
    hidden_grad = dot(g_own, wd_own[...], COLS1) + dot(g_oth, wd_oth[...], COLS1)
    gate_term = (hidden_grad * up * sig * (1.0 + gate * (1.0 - sig))).astype(B16)
    up_term = (hidden_grad * act).astype(B16)
    hidden_ref[...] = hidden
    gate_term_ref[...] = gate_term
    up_term_ref[...] = up_term
    copies[2].wait()
    copies[3].wait()
    give_ref[...] = results(cap, hidden, gate_term, up_term, wd_oth, wg, wu)


def keep_kernel(
    cap, side_ref, hidden_ref, gate_term_ref, up_term_ref, wg_far, wu_far, wd_far,
    keep_ref, wd, wg, wu, sems,
):
    _, here, _ = halves(side_ref, wd.shape[1])
    copies = fetch(
        [(wd_far.at[:, here], wd), (wg_far.at[here], wg), (wu_far.at[here], wu)], sems
    )
    for c in copies:
        c.wait()
    keep_ref[...] = results(cap, hidden_ref[...], gate_term_ref[...], up_term_ref[...], wd, wg, wu)


def down_kernel(bit_ref, packs_ref, cols_ref, keep_ref, give_ref):
    n = keep_ref.shape[1]
    slots = packs_ref.shape[1]
    wide = cols_ref.shape[2]
    bit = bit_ref[0]
    for at, out in ((1 - bit, give_ref), (bit, keep_ref)):
        cols = pl.ds(pl.multiple_of(at * n, n), n)
        for h in range(2):
            total = None
            for k in range(NX):
                rows = cols_ref[k, h * slots : (h + 1) * slots, cols]
                part = dot(rows, packs_ref[k, :, wide:], ROWS0)
                total = part if total is None else total + part
            out[h] = total.astype(B16)


def partner(bit_ref, pair_ref, h, at, n):
    start = (1 - bit_ref[0]) * (pair_ref.shape[1] // 2) + at
    return pair_ref[h, pl.ds(pl.multiple_of(start, n), n), :].astype(F32)


def halve_rows_kernel(last_ref, bit_ref, mine_ref, pair_ref, keep_ref, give_ref):
    n = keep_ref.shape[1]
    bit = bit_ref[0]
    for side, out in ((1 - bit, give_ref), (bit, keep_ref)):
        for h in range(2):
            mine = mine_ref[h, pl.ds(pl.multiple_of(side * n, n), n), :].astype(F32)
            out[h] = (mine + partner(last_ref, pair_ref, h, side * n, n)).astype(B16)


def halve_sides_kernel(last_ref, bit_ref, mine_ref, pair_ref, keep_ref, give_ref):
    n = keep_ref.shape[1]
    bit = bit_ref[0]
    for side, out in ((1 - bit, give_ref), (bit, keep_ref)):
        both = mine_ref[side].astype(F32) + partner(last_ref, pair_ref, side, 0, 2 * n)
        both = both.astype(B16)
        out[0] = both[0:n]
        out[1] = both[n : 2 * n]


def per_device(tokens, expert_ids, route_weight, gate_weight, up_weight, down_weight, cotangent):
    owners = lax.axis_size("expert")
    tok_rows, choose = expert_ids.shape
    cap = 3 * tok_rows * choose // (2 * EXPERTS)
    half = tokens.shape[1]
    slots = owners * cap
    ff = gate_weight.shape[2]
    bf = lambda *shape: jax.ShapeDtypeStruct(shape, B16)
    side = lax.axis_index("tensor").astype(jnp.int32).reshape(1)
    bits = [lax.axis_index(a).astype(jnp.int32).reshape(1) for a in ("y1", "y2", "y4")]
    ids_t, w_t = expert_ids.T, route_weight.T
    (send,) = fused(
        functools.partial(dispatch_kernel, owners, cap),
        [bf(2 * slots, half)],
        hbm(ids_t),
        hbm(w_t),
        hbm(tokens),
        hbm(cotangent),
        flops=4 * slots * tok_rows * half * 2,
        far=range(4),
        scratch=landing(ids_t, w_t, tokens, cotangent),
    )
    high, low, right = fused(
        functools.partial(plan_kernel, owners, cap),
        [bf(tok_rows, 2 * slots)] * 3,
        hbm(ids_t),
        hbm(w_t),
        flops=tok_rows**3,
    )

    def trade(rows, axis, *shape):
        return lax.all_to_all(rows.reshape(shape), axis, split_axis=0, concat_axis=0, tiled=True)

    def swap(v):
        return lax.ppermute(v, "tensor", [(0, 1), (1, 0)])

    def pair(v, axis):
        return lax.all_gather(v, axis, axis=1, tiled=True)

    chunks = (owners, 2 * cap, half)
    own = trade(send, "expert", *chunks).reshape(2 * slots, half)
    oth = swap(own)
    floats = jax.ShapeDtypeStruct((slots, ff), F32)
    halfway = landing(bf(half, ff))
    gate, up, cols = fused(
        functools.partial(own_kernel, cap),
        [floats, floats, bf(NX, slots, half // NX)],
        side,
        own,
        gate_weight[0],
        hbm(up_weight[0]),
        scalars=1,
        flops=slots * half * 2 * ff * 2 + slots * 2 * slots * half * 4,
        mib=12,
        far=(3,),
        scratch=halfway,
    )
    gate, up, pack = fused(
        functools.partial(rest_kernel, cap),
        [floats, floats, pltpu.HBM((NX, slots, half // NX + ff), B16)],
        side,
        oth,
        gate,
        up,
        cols,
        gate_weight[0],
        hbm(up_weight[0]),
        scalars=1,
        flops=slots * half * 2 * ff * 2 + slots * 2 * slots * half * 2,
        mib=12,
        far=(6,),
        scratch=halfway,
        alias={2: 0, 3: 1},
    )
    packs = trade(pack, "x", *pack.shape)
    weights = [hbm(w[0]) for w in (gate_weight, up_weight, down_weight)]
    down_half, in_half = bf(ff, half), bf(half, ff)
    give, *terms = fused(
        functools.partial(give_kernel, cap),
        [bf(2 * slots, half)] + [bf(slots, ff)] * 3,
        side,
        own,
        oth,
        gate,
        up,
        *weights,
        scalars=1,
        flops=slots * half * 2 * ff * 5 + slots * 2 * slots * half * 8,
        mib=16,
        far=(5, 6, 7),
        scratch=landing(down_half, down_half, in_half, in_half),
    )
    got = swap(give)
    (keep,) = fused(
        functools.partial(keep_kernel, cap),
        [bf(2 * slots, half)],
        side,
        *terms,
        *weights,
        scalars=1,
        flops=slots * half * 2 * ff * 3 + slots * 2 * slots * half * 4,
        mib=12,
        far=(4, 5, 6),
        scratch=landing(down_half, in_half, in_half),
    )
    total = (keep.astype(F32) + got.astype(F32)).astype(B16)
    back = trade(total, "expert", *chunks).reshape(2 * slots, half)
    keep, give = fused(
        down_kernel,
        [bf(2, half // 8, ff)] * 2,
        bits[0],
        packs,
        pair(packs[:, :, : half // NX], "tensor"),
        scalars=1,
        flops=half // 2 * ff * slots * 2 * NX,
    )
    for step, kernel in ((1, halve_rows_kernel), (2, halve_sides_kernel)):
        keep, give = fused(
            kernel,
            [bf(2, keep.shape[1] // 2, ff)] * 2,
            bits[step - 1],
            bits[step],
            keep,
            pair(give, ("y1", "y2")[step - 1]),
            scalars=2,
        )
    mixed, token_grad, down_grad = fused(
        combine_kernel,
        [bf(tok_rows, half)] * 2 + [bf(half // 16, ff)],
        bits[2],
        high,
        low,
        right,
        back,
        keep,
        pair(give, "y4"),
        scalars=1,
        flops=tok_rows * 2 * slots * half * 6,
    )
    return mixed, token_grad, down_grad.T[None]


def solution(mesh):
    dp, owners, tensor = (mesh.shape[a] for a in ("dp", "expert", "tensor"))
    mesh = jax.sharding.Mesh(
        mesh.devices.reshape(2, 2, dp // (4 * NX), NX, owners, tensor),
        ("y4", "y2", "y1", "x", "expert", "tensor"),
    )
    ways = ("y4", "y2", "y1", "x")
    blocks = (*ways, "expert")
    placed = (
        P(blocks, "tensor"),
        P(blocks, None),
        P(blocks, None),
        P("expert", None, "tensor"),
        P("expert", None, "tensor"),
        P("expert", "tensor", None),
        P(blocks, "tensor"),
    )

    return jax.shard_map(
        per_device,
        mesh=mesh,
        in_specs=placed,
        out_specs=(P(blocks, "tensor"), P(blocks, "tensor"), P("expert", "tensor", ways)),
        check_vma=False,
    )
```

```python
import functools
import math

import jax
import jax.numpy as jnp
from jax import lax
from jax.experimental import pallas as pl
from jax.experimental.pallas import tpu as pltpu
from jax.sharding import PartitionSpec as P

EXPERTS = 128
NX = 4
B16 = jnp.bfloat16
F32 = jnp.float32
ROWS0 = (((0,), (0,)), ((), ()))
COLS1 = (((1,), (1,)), ((), ()))


def dot(a, b, dims=None):
    if dims is None:
        dims = (((1,), (0,)), ((), ()))
    return lax.dot_general(a, b, dims, preferred_element_type=F32)


def hbm(v):
    return pltpu.with_memory_space_constraint(v, pltpu.HBM)


def fused(kernel, outs, *args, scalars=0, flops=0, mib=8, far=(), scratch=(), alias=None):
    specs = [
        pl.BlockSpec(
            memory_space=pltpu.SMEM if i < scalars else pltpu.HBM if i in far else pltpu.VMEM
        )
        for i in range(len(args))
    ]
    nbytes = sum(math.prod(a.shape) * a.dtype.itemsize for a in list(args) + list(outs))
    return pl.pallas_call(
        kernel,
        out_shape=outs,
        in_specs=specs,
        out_specs=[pl.BlockSpec(memory_space=pltpu.VMEM)] * len(outs),
        scratch_shapes=scratch,
        input_output_aliases=alias or {},
        compiler_params=pltpu.CompilerParams(vmem_limit_bytes=mib << 20),
        cost_estimate=pl.CostEstimate(flops=flops, bytes_accessed=nbytes, transcendentals=0),
    )(*args)


def fetch(pairs, sems):
    copies = [pltpu.make_async_copy(a, b, sems.at[i]) for i, (a, b) in enumerate(pairs)]
    for c in copies:
        c.start()
    return copies


def landing(*shapes):
    return [pltpu.VMEM(v.shape, v.dtype) for v in shapes] + [
        pltpu.SemaphoreType.DMA((len(shapes),))
    ]


def routing(ids_ref, w_ref, owners, cap):
    choose, toks = ids_ref.shape
    expert = lax.broadcasted_iota(jnp.int32, (owners, toks), 0)
    mask = jnp.zeros((owners, toks), F32)
    weight = jnp.zeros((owners, toks), F32)
    for k in range(choose):
        hit = ids_ref[k : k + 1, :] == expert
        mask = mask + jnp.where(hit, 1.0, 0.0)
        weight = weight + jnp.where(hit, w_ref[k : k + 1, :], 0.0)
    earlier = lax.broadcasted_iota(jnp.int32, (toks, toks), 0) < lax.broadcasted_iota(
        jnp.int32, (toks, toks), 1
    )
    rank = dot(mask.astype(B16), jnp.where(earlier, 1.0, 0.0).astype(B16))
    code = jnp.where(mask > 0.0, rank, -100.0)
    shape = (owners, 2 * cap, toks)
    code = jnp.broadcast_to(code[:, None, :], shape)
    weight = jnp.broadcast_to(weight[:, None, :], shape)
    row = lax.broadcasted_iota(jnp.int32, shape, 1).astype(F32)
    flat = (owners * 2 * cap, toks)
    left = jnp.where(code == row, 1.0, 0.0).reshape(flat)
    right = jnp.where(code == row - float(cap), 1.0, 0.0).reshape(flat)
    return left, right, weight.reshape(flat)


def dispatch_kernel(owners, cap, *refs):
    sources, out_ref, landed, sems = refs[:4], refs[4], refs[5:9], refs[9]
    copies = fetch(list(zip(sources, landed, strict=True)), sems)
    ids_ref, w_ref, tok_ref, cot_ref = landed
    copies[0].wait()
    copies[1].wait()
    left, right, weight = routing(ids_ref, w_ref, owners, cap)
    scale = jnp.sum(right * weight, axis=1, keepdims=True)
    left, right = left.astype(B16), right.astype(B16)
    copies[2].wait()
    copies[3].wait()
    out_ref[...] = (dot(left, tok_ref[...]) + dot(right, cot_ref[...]) * scale).astype(B16)


def plan_kernel(owners, cap, ids_ref, w_ref, high_ref, low_ref, right_ref):
    left, right, weight = routing(ids_ref, w_ref, owners, cap)
    left = (left * weight).T
    high = left.astype(B16)
    high_ref[...] = high
    low_ref[...] = (left - high.astype(F32)).astype(B16)
    right_ref[...] = right.T.astype(B16)


def combine_kernel(
    bit_ref, high_ref, low_ref, right_ref, rows_ref, mine_ref, pair_ref, mixed_ref, grad_ref, down_ref
):
    n = mine_ref.shape[1]
    for h in range(2):
        both = mine_ref[h].astype(F32) + partner(bit_ref, pair_ref, h, 0, n)
        down_ref[h * n : (h + 1) * n, :] = both.astype(B16)
    rows = rows_ref[...]
    mixed_ref[...] = (dot(high_ref[...], rows) + dot(low_ref[...], rows)).astype(B16)
    grad_ref[...] = dot(right_ref[...], rows).astype(B16)


def pick(shape, axis, cap, shift):
    compact = lax.broadcasted_iota(jnp.int32, shape, axis).astype(F32)
    chunk = lax.broadcasted_iota(jnp.int32, shape, 1 - axis).astype(F32)
    block = jnp.floor((compact + 0.5) * (1.0 / cap))
    return jnp.where(chunk == compact + cap * block + shift, 1.0, 0.0).astype(B16)


def halves(side_ref, half):
    side = side_ref[0]
    here = pl.ds(pl.multiple_of(side * half, half), half)
    there = pl.ds(pl.multiple_of((1 - side) * half, half), half)
    return side, here, there


def own_kernel(cap, side_ref, own_ref, wg_ref, wu_far, gate_ref, up_ref, cols_ref, wu, sems):
    rows, half = own_ref.shape
    slots = rows // 2
    _, here, _ = halves(side_ref, half)
    copies = fetch([(wu_far.at[here], wu)], sems)
    own = own_ref[...]
    x = dot(pick((slots, rows), 0, cap, 0), own).astype(B16)
    g = dot(pick((slots, rows), 0, cap, cap), own).astype(B16)
    wide = cols_ref.shape[2]
    for way in range(2 * NX):
        starts = [(y * NX + way % NX) * 64 for y in range(way // NX, wide // 32, 2)]
        cols_ref[way] = jnp.concatenate([g[:, at : at + 64] for at in starts], axis=1)
    gate_ref[...] = dot(x, wg_ref[here, :])
    copies[0].wait()
    up_ref[...] = dot(x, wu[...])


def rest_kernel(
    cap, side_ref, oth_ref, gate_in, up_in, cols_ref, wg_ref, wu_far, gate_ref, up_ref, pack_ref, wu, sems
):
    rows, half = oth_ref.shape
    slots = rows // 2
    _, _, there = halves(side_ref, half)
    copies = fetch([(wu_far.at[there], wu)], sems)
    wide = cols_ref.shape[2]
    x = dot(pick((slots, rows), 0, cap, 0), oth_ref[...]).astype(B16)
    pack_ref[:, :, 0:wide] = cols_ref[...]
    gate = gate_in[...] + dot(x, wg_ref[there, :])
    copies[0].wait()
    up = up_in[...] + dot(x, wu[...])
    hidden = (gate * (1.0 / (1.0 + jnp.exp(-gate))) * up).astype(B16)
    gate_ref[...] = gate
    up_ref[...] = up
    for way in range(2 * NX):
        pack_ref[way, :, wide:] = hidden


def results(cap, hidden, gate_term, up_term, wd, wg, wu):
    slots = hidden.shape[0]
    out_rows = dot(hidden, wd[...]).astype(B16)
    row_grad = (dot(gate_term, wg[...], COLS1) + dot(up_term, wu[...], COLS1)).astype(B16)
    from_x = pick((2 * slots, slots), 1, cap, 0)
    from_g = pick((2 * slots, slots), 1, cap, cap)
    return (dot(from_x, out_rows) + dot(from_g, row_grad)).astype(B16)


def give_kernel(
    cap, side_ref, own_ref, oth_ref, gate_ref, up_ref, wg_far, wu_far, wd_far,
    give_ref, hidden_ref, gate_term_ref, up_term_ref, wd_own, wd_oth, wg, wu, sems,
):
    rows, half = own_ref.shape
    slots = rows // 2
    _, here, there = halves(side_ref, half)
    copies = fetch(
        [
            (wd_far.at[:, here], wd_own),
            (wd_far.at[:, there], wd_oth),
            (wg_far.at[there], wg),
            (wu_far.at[there], wu),
        ],
        sems,
    )
    to_g = pick((slots, rows), 0, cap, cap)
    g_own, g_oth = dot(to_g, own_ref[...]).astype(B16), dot(to_g, oth_ref[...]).astype(B16)
    gate, up = gate_ref[...], up_ref[...]
    sig = 1.0 / (1.0 + jnp.exp(-gate))
    act = gate * sig
    hidden = (act * up).astype(B16)
    copies[0].wait()
    copies[1].wait()
    hidden_grad = dot(g_own, wd_own[...], COLS1) + dot(g_oth, wd_oth[...], COLS1)
    gate_term = (hidden_grad * up * sig * (1.0 + gate * (1.0 - sig))).astype(B16)
    up_term = (hidden_grad * act).astype(B16)
    hidden_ref[...] = hidden
    gate_term_ref[...] = gate_term
    up_term_ref[...] = up_term
    copies[2].wait()
    copies[3].wait()
    give_ref[...] = results(cap, hidden, gate_term, up_term, wd_oth, wg, wu)


def keep_kernel(
    cap, side_ref, hidden_ref, gate_term_ref, up_term_ref, wg_far, wu_far, wd_far,
    keep_ref, wd, wg, wu, sems,
):
    _, here, _ = halves(side_ref, wd.shape[1])
    copies = fetch(
        [(wd_far.at[:, here], wd), (wg_far.at[here], wg), (wu_far.at[here], wu)], sems
    )
    for c in copies:
        c.wait()
    keep_ref[...] = results(cap, hidden_ref[...], gate_term_ref[...], up_term_ref[...], wd, wg, wu)


def down_kernel(bit_ref, packs_ref, cols_ref, keep_ref, give_ref, sum_ref):
    n = keep_ref.shape[1]
    slots = packs_ref.shape[1]
    wide = cols_ref.shape[2]
    bit = bit_ref[0]
    for h in range(2):
        total = None
        for k in range(2 * NX):
            rows = cols_ref[k, h * slots : (h + 1) * slots, :]
            part = dot(rows, packs_ref[k, :, wide:], ROWS0)
            total = part if total is None else total + part
        sum_ref[...] = total
        give_ref[h] = sum_ref[pl.ds(pl.multiple_of((1 - bit) * n, n), n), :].astype(B16)
        keep_ref[h] = sum_ref[pl.ds(pl.multiple_of(bit * n, n), n), :].astype(B16)


def partner(bit_ref, pair_ref, h, at, n):
    start = (1 - bit_ref[0]) * (pair_ref.shape[1] // 2) + at
    return pair_ref[h, pl.ds(pl.multiple_of(start, n), n), :].astype(F32)


def halve_sides_kernel(last_ref, bit_ref, mine_ref, pair_ref, keep_ref, give_ref):
    n = keep_ref.shape[1]
    bit = bit_ref[0]
    for side, out in ((1 - bit, give_ref), (bit, keep_ref)):
        both = mine_ref[side].astype(F32) + partner(last_ref, pair_ref, side, 0, 2 * n)
        both = both.astype(B16)
        out[0] = both[0:n]
        out[1] = both[n : 2 * n]


def per_device(tokens, expert_ids, route_weight, gate_weight, up_weight, down_weight, cotangent):
    owners = lax.axis_size("expert")
    tok_rows, choose = expert_ids.shape
    cap = 3 * tok_rows * choose // (2 * EXPERTS)
    half = tokens.shape[1]
    slots = owners * cap
    ff = gate_weight.shape[2]
    bf = lambda *shape: jax.ShapeDtypeStruct(shape, B16)
    side = lax.axis_index("tensor").astype(jnp.int32).reshape(1)
    bits = [lax.axis_index(a).astype(jnp.int32).reshape(1) for a in ("y1", "y2", "y4")]
    ids_t, w_t = expert_ids.T, route_weight.T
    (send,) = fused(
        functools.partial(dispatch_kernel, owners, cap),
        [bf(2 * slots, half)],
        hbm(ids_t),
        hbm(w_t),
        hbm(tokens),
        hbm(cotangent),
        flops=4 * slots * tok_rows * half * 2,
        far=range(4),
        scratch=landing(ids_t, w_t, tokens, cotangent),
    )
    high, low, right = fused(
        functools.partial(plan_kernel, owners, cap),
        [bf(tok_rows, 2 * slots)] * 3,
        hbm(ids_t),
        hbm(w_t),
        flops=tok_rows**3,
    )

    def trade(rows, axis, *shape):
        return lax.all_to_all(rows.reshape(shape), axis, split_axis=0, concat_axis=0, tiled=True)

    def swap(v):
        return lax.ppermute(v, "tensor", [(0, 1), (1, 0)])

    def pair(v, axis):
        return lax.all_gather(v, axis, axis=1, tiled=True)

    chunks = (owners, 2 * cap, half)
    own = trade(send, "expert", *chunks).reshape(2 * slots, half)
    oth = swap(own)
    floats = jax.ShapeDtypeStruct((slots, ff), F32)
    halfway = landing(bf(half, ff))
    gate, up, cols = fused(
        functools.partial(own_kernel, cap),
        [floats, floats, bf(2 * NX, slots, half // (2 * NX))],
        side,
        own,
        gate_weight[0],
        hbm(up_weight[0]),
        scalars=1,
        flops=slots * half * 2 * ff * 2 + slots * 2 * slots * half * 4,
        mib=12,
        far=(3,),
        scratch=halfway,
    )
    gate, up, pack = fused(
        functools.partial(rest_kernel, cap),
        [floats, floats, pltpu.HBM((2 * NX, slots, half // (2 * NX) + ff), B16)],
        side,
        oth,
        gate,
        up,
        cols,
        gate_weight[0],
        hbm(up_weight[0]),
        scalars=1,
        flops=slots * half * 2 * ff * 2 + slots * 2 * slots * half * 2,
        mib=12,
        far=(6,),
        scratch=halfway,
        alias={2: 0, 3: 1},
    )
    packs = trade(pack, ("y1", "x"), *pack.shape)
    weights = [hbm(w[0]) for w in (gate_weight, up_weight, down_weight)]
    down_half, in_half = bf(ff, half), bf(half, ff)
    give, *terms = fused(
        functools.partial(give_kernel, cap),
        [bf(2 * slots, half)] + [bf(slots, ff)] * 3,
        side,
        own,
        oth,
        gate,
        up,
        *weights,
        scalars=1,
        flops=slots * half * 2 * ff * 5 + slots * 2 * slots * half * 8,
        mib=16,
        far=(5, 6, 7),
        scratch=landing(down_half, down_half, in_half, in_half),
    )
    got = swap(give)
    (keep,) = fused(
        functools.partial(keep_kernel, cap),
        [bf(2 * slots, half)],
        side,
        *terms,
        *weights,
        scalars=1,
        flops=slots * half * 2 * ff * 3 + slots * 2 * slots * half * 4,
        mib=12,
        far=(4, 5, 6),
        scratch=landing(down_half, in_half, in_half),
    )
    total = (keep.astype(F32) + got.astype(F32)).astype(B16)
    back = trade(total, "expert", *chunks).reshape(2 * slots, half)
    keep, give = fused(
        down_kernel,
        [bf(2, half // 16, ff)] * 2,
        bits[1],
        packs,
        pair(packs[:, :, : half // (2 * NX)], "tensor"),
        scalars=1,
        flops=half // 4 * ff * slots * 4 * NX,
        scratch=[pltpu.VMEM((half // 8, ff), F32)],
    )
    keep, give = fused(
        halve_sides_kernel,
        [bf(2, half // 32, ff)] * 2,
        bits[1],
        bits[2],
        keep,
        pair(give, "y2"),
        scalars=2,
    )
    mixed, token_grad, down_grad = fused(
        combine_kernel,
        [bf(tok_rows, half)] * 2 + [bf(half // 16, ff)],
        bits[2],
        high,
        low,
        right,
        back,
        keep,
        pair(give, "y4"),
        scalars=1,
        flops=tok_rows * 2 * slots * half * 6,
    )
    return mixed, token_grad, down_grad.T[None]


def solution(mesh):
    dp, owners, tensor = (mesh.shape[a] for a in ("dp", "expert", "tensor"))
    mesh = jax.sharding.Mesh(
        mesh.devices.reshape(2, 2, dp // (4 * NX), NX, owners, tensor),
        ("y4", "y2", "y1", "x", "expert", "tensor"),
    )
    ways = ("y4", "y2", "y1", "x")
    blocks = (*ways, "expert")
    placed = (
        P(blocks, "tensor"),
        P(blocks, None),
        P(blocks, None),
        P("expert", None, "tensor"),
        P("expert", None, "tensor"),
        P("expert", "tensor", None),
        P(blocks, "tensor"),
    )

    return jax.shard_map(
        per_device,
        mesh=mesh,
        in_specs=placed,
        out_specs=(P(blocks, "tensor"), P(blocks, "tensor"), P("expert", "tensor", ways)),
        check_vma=False,
    )
```

```python
import functools
import math

import jax
import jax.numpy as jnp
from jax import lax
from jax.experimental import pallas as pl
from jax.experimental.pallas import tpu as pltpu
from jax.sharding import PartitionSpec as P

EXPERTS = 128
NX = 4
B16 = jnp.bfloat16
F32 = jnp.float32
ROWS0 = (((0,), (0,)), ((), ()))
COLS1 = (((1,), (1,)), ((), ()))


def dot(a, b, dims=None):
    if dims is None:
        dims = (((1,), (0,)), ((), ()))
    return lax.dot_general(a, b, dims, preferred_element_type=F32)


def hbm(v):
    return pltpu.with_memory_space_constraint(v, pltpu.HBM)


def fused(kernel, outs, *args, scalars=0, flops=0, mib=8, far=(), scratch=(), alias=None):
    specs = [
        pl.BlockSpec(
            memory_space=pltpu.SMEM if i < scalars else pltpu.HBM if i in far else pltpu.VMEM
        )
        for i in range(len(args))
    ]
    nbytes = sum(math.prod(a.shape) * a.dtype.itemsize for a in list(args) + list(outs))
    return pl.pallas_call(
        kernel,
        out_shape=outs,
        in_specs=specs,
        out_specs=[pl.BlockSpec(memory_space=pltpu.VMEM)] * len(outs),
        scratch_shapes=scratch,
        input_output_aliases=alias or {},
        compiler_params=pltpu.CompilerParams(vmem_limit_bytes=mib << 20),
        cost_estimate=pl.CostEstimate(flops=flops, bytes_accessed=nbytes, transcendentals=0),
    )(*args)


def fetch(pairs, sems):
    copies = [pltpu.make_async_copy(a, b, sems.at[i]) for i, (a, b) in enumerate(pairs)]
    for c in copies:
        c.start()
    return copies


def landing(*shapes):
    return [pltpu.VMEM(v.shape, v.dtype) for v in shapes] + [
        pltpu.SemaphoreType.DMA((len(shapes),))
    ]


def routing(ids_ref, w_ref, owners, cap):
    choose, toks = ids_ref.shape
    expert = lax.broadcasted_iota(jnp.int32, (owners, toks), 0)
    mask = jnp.zeros((owners, toks), F32)
    weight = jnp.zeros((owners, toks), F32)
    for k in range(choose):
        hit = ids_ref[k : k + 1, :] == expert
        mask = mask + jnp.where(hit, 1.0, 0.0)
        weight = weight + jnp.where(hit, w_ref[k : k + 1, :], 0.0)
    earlier = lax.broadcasted_iota(jnp.int32, (toks, toks), 0) < lax.broadcasted_iota(
        jnp.int32, (toks, toks), 1
    )
    rank = dot(mask.astype(B16), jnp.where(earlier, 1.0, 0.0).astype(B16))
    code = jnp.where(mask > 0.0, rank, -100.0)
    shape = (owners, 2 * cap, toks)
    code = jnp.broadcast_to(code[:, None, :], shape)
    weight = jnp.broadcast_to(weight[:, None, :], shape)
    row = lax.broadcasted_iota(jnp.int32, shape, 1).astype(F32)
    flat = (owners * 2 * cap, toks)
    left = jnp.where(code == row, 1.0, 0.0).reshape(flat)
    right = jnp.where(code == row - float(cap), 1.0, 0.0).reshape(flat)
    return left, right, weight.reshape(flat)


def dispatch_kernel(owners, cap, *refs):
    sources, out_ref, landed, sems = refs[:4], refs[4], refs[5:9], refs[9]
    copies = fetch(list(zip(sources, landed, strict=True)), sems)
    ids_ref, w_ref, tok_ref, cot_ref = landed
    copies[0].wait()
    copies[1].wait()
    left, right, weight = routing(ids_ref, w_ref, owners, cap)
    scale = jnp.sum(right * weight, axis=1, keepdims=True)
    left, right = left.astype(B16), right.astype(B16)
    copies[2].wait()
    copies[3].wait()
    out_ref[...] = (dot(left, tok_ref[...]) + dot(right, cot_ref[...]) * scale).astype(B16)


def plan_kernel(owners, cap, ids_ref, w_ref, high_ref, low_ref, right_ref):
    left, right, weight = routing(ids_ref, w_ref, owners, cap)
    left = (left * weight).T
    high = left.astype(B16)
    high_ref[...] = high
    low_ref[...] = (left - high.astype(F32)).astype(B16)
    right_ref[...] = right.T.astype(B16)


def combine_kernel(
    bit_ref, high_ref, low_ref, right_ref, rows_ref, mine_ref, pair_ref, mixed_ref, grad_ref, down_ref
):
    n = mine_ref.shape[1]
    for h in range(2):
        both = mine_ref[h].astype(F32) + partner(bit_ref, pair_ref, h, 0, n)
        down_ref[h * n : (h + 1) * n, :] = both.astype(B16)
    rows = rows_ref[...]
    mixed_ref[...] = (dot(high_ref[...], rows) + dot(low_ref[...], rows)).astype(B16)
    grad_ref[...] = dot(right_ref[...], rows).astype(B16)


def pick(shape, axis, cap, shift):
    compact = lax.broadcasted_iota(jnp.int32, shape, axis).astype(F32)
    chunk = lax.broadcasted_iota(jnp.int32, shape, 1 - axis).astype(F32)
    block = jnp.floor((compact + 0.5) * (1.0 / cap))
    return jnp.where(chunk == compact + cap * block + shift, 1.0, 0.0).astype(B16)


def halves(side_ref, half):
    side = side_ref[0]
    here = pl.ds(pl.multiple_of(side * half, half), half)
    there = pl.ds(pl.multiple_of((1 - side) * half, half), half)
    return side, here, there


def own_kernel(
    cap, side_ref, own_ref, wg_far, wu_far, gate_ref, up_ref, cols_ref, wg_oth, wu_oth, wg, wu, sems
):
    rows, half = own_ref.shape
    slots = rows // 2
    _, here, there = halves(side_ref, half)
    copies = fetch(
        [
            (wg_far.at[here], wg),
            (wu_far.at[here], wu),
            (wg_far.at[there], wg_oth),
            (wu_far.at[there], wu_oth),
        ],
        sems,
    )
    own = own_ref[...]
    x = dot(pick((slots, rows), 0, cap, 0), own).astype(B16)
    g = dot(pick((slots, rows), 0, cap, cap), own).astype(B16)
    wide = half // NX
    for xd in range(NX):
        cols = [g[:, (y * NX + xd) * 64 : (y * NX + xd) * 64 + 64] for y in range(wide // 64)]
        cols_ref[xd, :, 0 : wide // 2] = jnp.concatenate(cols[0::2], axis=1)
        cols_ref[xd, :, wide // 2 : wide] = jnp.concatenate(cols[1::2], axis=1)
    copies[0].wait()
    gate_ref[...] = dot(x, wg[...])
    copies[1].wait()
    up_ref[...] = dot(x, wu[...])
    copies[2].wait()
    copies[3].wait()


def rest_kernel(cap, oth_ref, gate_in, up_in, cols_ref, wg_ref, wu_ref, gate_ref, up_ref, pack_ref):
    rows = oth_ref.shape[0]
    slots = rows // 2
    wide = cols_ref.shape[2]
    x = dot(pick((slots, rows), 0, cap, 0), oth_ref[...]).astype(B16)
    gate = gate_in[...] + dot(x, wg_ref[...])
    up = up_in[...] + dot(x, wu_ref[...])
    hidden = (gate * (1.0 / (1.0 + jnp.exp(-gate))) * up).astype(B16)
    gate_ref[...] = gate
    up_ref[...] = up
    pack_ref[:, :, 0:wide] = cols_ref[...]
    for xd in range(NX):
        pack_ref[xd, :, wide:] = hidden


def results(cap, hidden, gate_term, up_term, wd, wg, wu):
    slots = hidden.shape[0]
    out_rows = dot(hidden, wd[...]).astype(B16)
    row_grad = (dot(gate_term, wg[...], COLS1) + dot(up_term, wu[...], COLS1)).astype(B16)
    from_x = pick((2 * slots, slots), 1, cap, 0)
    from_g = pick((2 * slots, slots), 1, cap, cap)
    return (dot(from_x, out_rows) + dot(from_g, row_grad)).astype(B16)


def give_kernel(
    cap, side_ref, own_ref, oth_ref, gate_ref, up_ref, wg_far, wu_far, wd_far,
    give_ref, hidden_ref, gate_term_ref, up_term_ref, wd_own, wd_oth, wg, wu, sems,
):
    rows, half = own_ref.shape
    slots = rows // 2
    _, here, there = halves(side_ref, half)
    copies = fetch(
        [
            (wd_far.at[:, here], wd_own),
            (wd_far.at[:, there], wd_oth),
            (wg_far.at[there], wg),
            (wu_far.at[there], wu),
        ],
        sems,
    )
    to_g = pick((slots, rows), 0, cap, cap)
    g_own, g_oth = dot(to_g, own_ref[...]).astype(B16), dot(to_g, oth_ref[...]).astype(B16)
    gate, up = gate_ref[...], up_ref[...]
    sig = 1.0 / (1.0 + jnp.exp(-gate))
    act = gate * sig
    hidden = (act * up).astype(B16)
    copies[0].wait()
    copies[1].wait()
    hidden_grad = dot(g_own, wd_own[...], COLS1) + dot(g_oth, wd_oth[...], COLS1)
    gate_term = (hidden_grad * up * sig * (1.0 + gate * (1.0 - sig))).astype(B16)
    up_term = (hidden_grad * act).astype(B16)
    hidden_ref[...] = hidden
    gate_term_ref[...] = gate_term
    up_term_ref[...] = up_term
    copies[2].wait()
    copies[3].wait()
    give_ref[...] = results(cap, hidden, gate_term, up_term, wd_oth, wg, wu)


def keep_kernel(
    cap, side_ref, hidden_ref, gate_term_ref, up_term_ref, wg_far, wu_far, wd_far,
    keep_ref, wd, wg, wu, sems,
):
    _, here, _ = halves(side_ref, wd.shape[1])
    copies = fetch(
        [(wd_far.at[:, here], wd), (wg_far.at[here], wg), (wu_far.at[here], wu)], sems
    )
    for c in copies:
        c.wait()
    keep_ref[...] = results(cap, hidden_ref[...], gate_term_ref[...], up_term_ref[...], wd, wg, wu)


def down_kernel(bit_ref, side_ref, packs_ref, oth_ref, keep_ref, give_ref):
    n = keep_ref.shape[1]
    wide = oth_ref.shape[2]
    bit, side = bit_ref[0], side_ref[0]
    for at, out in ((1 - bit, give_ref), (bit, keep_ref)):
        cols = pl.ds(pl.multiple_of(at * n, n), n)
        for place, ref in ((side, packs_ref), (1 - side, oth_ref)):
            total = None
            for k in range(NX):
                part = dot(ref[k, :, cols], packs_ref[k, :, wide:], ROWS0)
                total = part if total is None else total + part
            out[place] = total.astype(B16)


def partner(bit_ref, pair_ref, h, at, n):
    start = (1 - bit_ref[0]) * (pair_ref.shape[1] // 2) + at
    return pair_ref[h, pl.ds(pl.multiple_of(start, n), n), :].astype(F32)


def halve_rows_kernel(last_ref, bit_ref, mine_ref, pair_ref, keep_ref, give_ref):
    n = keep_ref.shape[1]
    bit = bit_ref[0]
    for side, out in ((1 - bit, give_ref), (bit, keep_ref)):
        for h in range(2):
            mine = mine_ref[h, pl.ds(pl.multiple_of(side * n, n), n), :].astype(F32)
            out[h] = (mine + partner(last_ref, pair_ref, h, side * n, n)).astype(B16)


def halve_sides_kernel(last_ref, bit_ref, mine_ref, pair_ref, keep_ref, give_ref):
    n = keep_ref.shape[1]
    bit = bit_ref[0]
    for side, out in ((1 - bit, give_ref), (bit, keep_ref)):
        both = mine_ref[side].astype(F32) + partner(last_ref, pair_ref, side, 0, 2 * n)
        both = both.astype(B16)
        out[0] = both[0:n]
        out[1] = both[n : 2 * n]


def per_device(tokens, expert_ids, route_weight, gate_weight, up_weight, down_weight, cotangent):
    owners = lax.axis_size("expert")
    tok_rows, choose = expert_ids.shape
    cap = 3 * tok_rows * choose // (2 * EXPERTS)
    half = tokens.shape[1]
    slots = owners * cap
    ff = gate_weight.shape[2]
    bf = lambda *shape: jax.ShapeDtypeStruct(shape, B16)
    side = lax.axis_index("tensor").astype(jnp.int32).reshape(1)
    bits = [lax.axis_index(a).astype(jnp.int32).reshape(1) for a in ("y1", "y2", "y4")]
    ids_t, w_t = expert_ids.T, route_weight.T
    (send,) = fused(
        functools.partial(dispatch_kernel, owners, cap),
        [bf(2 * slots, half)],
        hbm(ids_t),
        hbm(w_t),
        hbm(tokens),
        hbm(cotangent),
        flops=4 * slots * tok_rows * half * 2,
        far=range(4),
        scratch=landing(ids_t, w_t, tokens, cotangent),
    )
    high, low, right = fused(
        functools.partial(plan_kernel, owners, cap),
        [bf(tok_rows, 2 * slots)] * 3,
        hbm(ids_t),
        hbm(w_t),
        flops=tok_rows**3,
    )

    def trade(rows, axis, *shape):
        return lax.all_to_all(rows.reshape(shape), axis, split_axis=0, concat_axis=0, tiled=True)

    def swap(v):
        return lax.ppermute(v, "tensor", [(0, 1), (1, 0)])

    def pair(v, axis):
        return lax.all_gather(v, axis, axis=1, tiled=True)

    chunks = (owners, 2 * cap, half)
    own = trade(send, "expert", *chunks).reshape(2 * slots, half)
    oth = swap(own)
    floats = jax.ShapeDtypeStruct((slots, ff), F32)
    down_half, in_half = bf(ff, half), bf(half, ff)
    weights = [hbm(w[0]) for w in (gate_weight, up_weight, down_weight)]
    gate, up, cols, wg_oth, wu_oth = fused(
        functools.partial(own_kernel, cap),
        [floats, floats, bf(NX, slots, half // NX), in_half, in_half],
        side,
        own,
        *weights[:2],
        scalars=1,
        flops=slots * half * 2 * ff * 2 + slots * 2 * slots * half * 4,
        mib=12,
        far=(2, 3),
        scratch=[pltpu.VMEM(in_half.shape, B16)] * 2 + [pltpu.SemaphoreType.DMA((4,))],
    )
    gate, up, pack = fused(
        functools.partial(rest_kernel, cap),
        [floats, floats, pltpu.HBM((NX, slots, half // NX + ff), B16)],
        oth,
        gate,
        up,
        cols,
        wg_oth,
        wu_oth,
        flops=slots * half * 2 * ff * 2 + slots * 2 * slots * half * 2,
        mib=12,
        alias={1: 0, 2: 1},
    )
    packs = trade(pack, "x", *pack.shape)
    give, *terms = fused(
        functools.partial(give_kernel, cap),
        [bf(2 * slots, half)] + [bf(slots, ff)] * 3,
        side,
        own,
        oth,
        gate,
        up,
        *weights,
        scalars=1,
        flops=slots * half * 2 * ff * 5 + slots * 2 * slots * half * 8,
        mib=16,
        far=(5, 6, 7),
        scratch=landing(down_half, down_half, in_half, in_half),
    )
    got = swap(give)
    (keep,) = fused(
        functools.partial(keep_kernel, cap),
        [bf(2 * slots, half)],
        side,
        *terms,
        *weights,
        scalars=1,
        flops=slots * half * 2 * ff * 3 + slots * 2 * slots * half * 4,
        mib=12,
        far=(4, 5, 6),
        scratch=landing(down_half, in_half, in_half),
    )
    total = (keep.astype(F32) + got.astype(F32)).astype(B16)
    cols_oth = swap(packs[:, :, : half // NX])
    back = trade(total, "expert", *chunks).reshape(2 * slots, half)
    keep, give = fused(
        down_kernel,
        [bf(2, half // 8, ff)] * 2,
        bits[0],
        side,
        packs,
        cols_oth,
        scalars=2,
        flops=half // 2 * ff * slots * 2 * NX,
    )
    for step, kernel in ((1, halve_rows_kernel), (2, halve_sides_kernel)):
        keep, give = fused(
            kernel,
            [bf(2, keep.shape[1] // 2, ff)] * 2,
            bits[step - 1],
            bits[step],
            keep,
            pair(give, ("y1", "y2")[step - 1]),
            scalars=2,
        )
    mixed, token_grad, down_grad = fused(
        combine_kernel,
        [bf(tok_rows, half)] * 2 + [bf(half // 16, ff)],
        bits[2],
        high,
        low,
        right,
        back,
        keep,
        pair(give, "y4"),
        scalars=1,
        flops=tok_rows * 2 * slots * half * 6,
    )
    return mixed, token_grad, down_grad.T[None]


def solution(mesh):
    dp, owners, tensor = (mesh.shape[a] for a in ("dp", "expert", "tensor"))
    mesh = jax.sharding.Mesh(
        mesh.devices.reshape(2, 2, dp // (4 * NX), NX, owners, tensor),
        ("y4", "y2", "y1", "x", "expert", "tensor"),
    )
    ways = ("y4", "y2", "y1", "x")
    blocks = (*ways, "expert")
    placed = (
        P(blocks, "tensor"),
        P(blocks, None),
        P(blocks, None),
        P("expert", None, "tensor"),
        P("expert", None, "tensor"),
        P("expert", "tensor", None),
        P(blocks, "tensor"),
    )

    return jax.shard_map(
        per_device,
        mesh=mesh,
        in_specs=placed,
        out_specs=(P(blocks, "tensor"), P(blocks, "tensor"), P("expert", "tensor", ways)),
        check_vma=False,
    )
```

```python
import functools
import math

import jax
import jax.numpy as jnp
from jax import lax
from jax.experimental import pallas as pl
from jax.experimental.pallas import tpu as pltpu
from jax.sharding import PartitionSpec as P

EXPERTS = 128
NX = 4
B16 = jnp.bfloat16
F32 = jnp.float32
ROWS0 = (((0,), (0,)), ((), ()))
COLS1 = (((1,), (1,)), ((), ()))


def dot(a, b, dims=None):
    if dims is None:
        dims = (((1,), (0,)), ((), ()))
    return lax.dot_general(a, b, dims, preferred_element_type=F32)


def hbm(v):
    return pltpu.with_memory_space_constraint(v, pltpu.HBM)


def fused(kernel, outs, *args, scalars=0, flops=0, mib=8, far=(), scratch=(), alias=None):
    specs = [
        pl.BlockSpec(
            memory_space=pltpu.SMEM if i < scalars else pltpu.HBM if i in far else pltpu.VMEM
        )
        for i in range(len(args))
    ]
    nbytes = sum(math.prod(a.shape) * a.dtype.itemsize for a in list(args) + list(outs))
    return pl.pallas_call(
        kernel,
        out_shape=outs,
        in_specs=specs,
        out_specs=[pl.BlockSpec(memory_space=pltpu.VMEM)] * len(outs),
        scratch_shapes=scratch,
        input_output_aliases=alias or {},
        compiler_params=pltpu.CompilerParams(vmem_limit_bytes=mib << 20),
        cost_estimate=pl.CostEstimate(flops=flops, bytes_accessed=nbytes, transcendentals=0),
    )(*args)


def fetch(pairs, sems):
    copies = [pltpu.make_async_copy(a, b, sems.at[i]) for i, (a, b) in enumerate(pairs)]
    for c in copies:
        c.start()
    return copies


def landing(*shapes):
    return [pltpu.VMEM(v.shape, v.dtype) for v in shapes] + [
        pltpu.SemaphoreType.DMA((len(shapes),))
    ]


def routing(ids_ref, w_ref, owners, cap):
    choose, toks = ids_ref.shape
    expert = lax.broadcasted_iota(jnp.int32, (owners, toks), 0)
    mask = jnp.zeros((owners, toks), F32)
    weight = jnp.zeros((owners, toks), F32)
    for k in range(choose):
        hit = ids_ref[k : k + 1, :] == expert
        mask = mask + jnp.where(hit, 1.0, 0.0)
        weight = weight + jnp.where(hit, w_ref[k : k + 1, :], 0.0)
    earlier = lax.broadcasted_iota(jnp.int32, (toks, toks), 0) < lax.broadcasted_iota(
        jnp.int32, (toks, toks), 1
    )
    rank = dot(mask.astype(B16), jnp.where(earlier, 1.0, 0.0).astype(B16))
    code = jnp.where(mask > 0.0, rank, -100.0)
    shape = (owners, 2 * cap, toks)
    code = jnp.broadcast_to(code[:, None, :], shape)
    weight = jnp.broadcast_to(weight[:, None, :], shape)
    row = lax.broadcasted_iota(jnp.int32, shape, 1).astype(F32)
    flat = (owners * 2 * cap, toks)
    left = jnp.where(code == row, 1.0, 0.0).reshape(flat)
    right = jnp.where(code == row - float(cap), 1.0, 0.0).reshape(flat)
    return left, right, weight.reshape(flat)


def dispatch_kernel(owners, cap, *refs):
    sources, out_ref, landed, sems = refs[:4], refs[4], refs[5:9], refs[9]
    copies = fetch(list(zip(sources, landed, strict=True)), sems)
    ids_ref, w_ref, tok_ref, cot_ref = landed
    copies[0].wait()
    copies[1].wait()
    left, right, weight = routing(ids_ref, w_ref, owners, cap)
    scale = jnp.sum(right * weight, axis=1, keepdims=True)
    left, right = left.astype(B16), right.astype(B16)
    copies[2].wait()
    copies[3].wait()
    out_ref[...] = (dot(left, tok_ref[...]) + dot(right, cot_ref[...]) * scale).astype(B16)


def plan_kernel(owners, cap, ids_ref, w_ref, high_ref, low_ref, right_ref):
    left, right, weight = routing(ids_ref, w_ref, owners, cap)
    left = (left * weight).T
    high = left.astype(B16)
    high_ref[...] = high
    low_ref[...] = (left - high.astype(F32)).astype(B16)
    right_ref[...] = right.T.astype(B16)


def combine_kernel(
    bit_ref, high_ref, low_ref, right_ref, rows_ref, mine_ref, pair_ref, mixed_ref, grad_ref, down_ref
):
    n = mine_ref.shape[1]
    for h in range(2):
        both = mine_ref[h].astype(F32) + partner(bit_ref, pair_ref, h, 0, n)
        down_ref[h * n : (h + 1) * n, :] = both.astype(B16)
    rows = rows_ref[...]
    mixed_ref[...] = (dot(high_ref[...], rows) + dot(low_ref[...], rows)).astype(B16)
    grad_ref[...] = dot(right_ref[...], rows).astype(B16)


def pick(shape, axis, cap, shift):
    compact = lax.broadcasted_iota(jnp.int32, shape, axis).astype(F32)
    chunk = lax.broadcasted_iota(jnp.int32, shape, 1 - axis).astype(F32)
    block = jnp.floor((compact + 0.5) * (1.0 / cap))
    return jnp.where(chunk == compact + cap * block + shift, 1.0, 0.0).astype(B16)


def halves(side_ref, half):
    side = side_ref[0]
    here = pl.ds(pl.multiple_of(side * half, half), half)
    there = pl.ds(pl.multiple_of((1 - side) * half, half), half)
    return side, here, there


def own_kernel(
    cap, side_ref, own_ref, wg_far, wu_far, gate_ref, up_ref, cols_ref, wg_oth, wu_oth, wg, wu, sems
):
    rows, half = own_ref.shape
    slots = rows // 2
    _, here, there = halves(side_ref, half)
    copies = fetch(
        [
            (wg_far.at[here], wg),
            (wu_far.at[here], wu),
            (wg_far.at[there], wg_oth),
            (wu_far.at[there], wu_oth),
        ],
        sems,
    )
    own = own_ref[...]
    x = dot(pick((slots, rows), 0, cap, 0), own).astype(B16)
    g = dot(pick((slots, rows), 0, cap, cap), own).astype(B16)
    wide = half // NX
    for xd in range(NX):
        cols = [g[:, (y * NX + xd) * 64 : (y * NX + xd) * 64 + 64] for y in range(wide // 64)]
        cols_ref[xd, :, 0 : wide // 2] = jnp.concatenate(cols[0::2], axis=1)
        cols_ref[xd, :, wide // 2 : wide] = jnp.concatenate(cols[1::2], axis=1)
    copies[0].wait()
    gate_ref[...] = dot(x, wg[...])
    copies[1].wait()
    up_ref[...] = dot(x, wu[...])
    copies[2].wait()
    copies[3].wait()


def rest_kernel(cap, oth_ref, gate_in, up_in, cols_ref, wg_ref, wu_ref, gate_ref, up_ref, pack_ref):
    rows = oth_ref.shape[0]
    slots = rows // 2
    wide = cols_ref.shape[2]
    x = dot(pick((slots, rows), 0, cap, 0), oth_ref[...]).astype(B16)
    gate = gate_in[...] + dot(x, wg_ref[...])
    up = up_in[...] + dot(x, wu_ref[...])
    hidden = (gate * (1.0 / (1.0 + jnp.exp(-gate))) * up).astype(B16)
    gate_ref[...] = gate
    up_ref[...] = up
    pack_ref[:, :, 0:wide] = cols_ref[...]
    for xd in range(NX):
        pack_ref[xd, :, wide:] = hidden


def results(cap, hidden, gate_term, up_term, wd, wg, wu):
    slots = hidden.shape[0]
    out_rows = dot(hidden, wd[...]).astype(B16)
    row_grad = (dot(gate_term, wg[...], COLS1) + dot(up_term, wu[...], COLS1)).astype(B16)
    from_x = pick((2 * slots, slots), 1, cap, 0)
    from_g = pick((2 * slots, slots), 1, cap, cap)
    return (dot(from_x, out_rows) + dot(from_g, row_grad)).astype(B16)


def give_kernel(
    cap, side_ref, own_ref, oth_ref, gate_ref, up_ref, wg_far, wu_far, wd_far,
    give_ref, hidden_ref, gate_term_ref, up_term_ref, wd_own, wd_oth, wg, wu, sems,
):
    rows, half = own_ref.shape
    slots = rows // 2
    _, here, there = halves(side_ref, half)
    copies = fetch(
        [
            (wd_far.at[:, here], wd_own),
            (wd_far.at[:, there], wd_oth),
            (wg_far.at[there], wg),
            (wu_far.at[there], wu),
        ],
        sems,
    )
    to_g = pick((slots, rows), 0, cap, cap)
    g_own, g_oth = dot(to_g, own_ref[...]).astype(B16), dot(to_g, oth_ref[...]).astype(B16)
    gate, up = gate_ref[...], up_ref[...]
    sig = 1.0 / (1.0 + jnp.exp(-gate))
    act = gate * sig
    hidden = (act * up).astype(B16)
    copies[0].wait()
    copies[1].wait()
    hidden_grad = dot(g_own, wd_own[...], COLS1) + dot(g_oth, wd_oth[...], COLS1)
    gate_term = (hidden_grad * up * sig * (1.0 + gate * (1.0 - sig))).astype(B16)
    up_term = (hidden_grad * act).astype(B16)
    hidden_ref[...] = hidden
    gate_term_ref[...] = gate_term
    up_term_ref[...] = up_term
    copies[2].wait()
    copies[3].wait()
    give_ref[...] = results(cap, hidden, gate_term, up_term, wd_oth, wg, wu)


def keep_kernel(
    cap, side_ref, hidden_ref, gate_term_ref, up_term_ref, wg_far, wu_far, wd_far,
    keep_ref, wd, wg, wu, sems,
):
    _, here, _ = halves(side_ref, wd.shape[1])
    copies = fetch(
        [(wd_far.at[:, here], wd), (wg_far.at[here], wg), (wu_far.at[here], wu)], sems
    )
    for c in copies:
        c.wait()
    keep_ref[...] = results(cap, hidden_ref[...], gate_term_ref[...], up_term_ref[...], wd, wg, wu)


def down_kernel(bit_ref, packs_ref, cols_ref, keep_ref, give_ref):
    n = keep_ref.shape[1]
    slots = packs_ref.shape[1]
    wide = cols_ref.shape[2]
    bit = bit_ref[0]
    for at, out in ((1 - bit, give_ref), (bit, keep_ref)):
        cols = pl.ds(pl.multiple_of(at * n, n), n)
        for h in range(2):
            total = None
            for k in range(NX):
                rows = cols_ref[k, h * slots : (h + 1) * slots, cols]
                part = dot(rows, packs_ref[k, :, wide:], ROWS0)
                total = part if total is None else total + part
            out[h] = total.astype(B16)


def partner(bit_ref, pair_ref, h, at, n):
    start = (1 - bit_ref[0]) * (pair_ref.shape[1] // 2) + at
    return pair_ref[h, pl.ds(pl.multiple_of(start, n), n), :].astype(F32)


def halve_rows_kernel(last_ref, bit_ref, mine_ref, pair_ref, keep_ref, give_ref):
    n = keep_ref.shape[1]
    bit = bit_ref[0]
    for side, out in ((1 - bit, give_ref), (bit, keep_ref)):
        for h in range(2):
            mine = mine_ref[h, pl.ds(pl.multiple_of(side * n, n), n), :].astype(F32)
            out[h] = (mine + partner(last_ref, pair_ref, h, side * n, n)).astype(B16)


def halve_sides_kernel(last_ref, bit_ref, mine_ref, pair_ref, keep_ref, give_ref):
    n = keep_ref.shape[1]
    bit = bit_ref[0]
    for side, out in ((1 - bit, give_ref), (bit, keep_ref)):
        both = mine_ref[side].astype(F32) + partner(last_ref, pair_ref, side, 0, 2 * n)
        both = both.astype(B16)
        out[0] = both[0:n]
        out[1] = both[n : 2 * n]


def per_device(tokens, expert_ids, route_weight, gate_weight, up_weight, down_weight, cotangent):
    owners = lax.axis_size("expert")
    tok_rows, choose = expert_ids.shape
    cap = 3 * tok_rows * choose // (2 * EXPERTS)
    half = tokens.shape[1]
    slots = owners * cap
    ff = gate_weight.shape[2]
    bf = lambda *shape: jax.ShapeDtypeStruct(shape, B16)
    side = lax.axis_index("tensor").astype(jnp.int32).reshape(1)
    bits = [lax.axis_index(a).astype(jnp.int32).reshape(1) for a in ("y1", "y2", "y4")]
    ids_t, w_t = expert_ids.T, route_weight.T
    (send,) = fused(
        functools.partial(dispatch_kernel, owners, cap),
        [bf(2 * slots, half)],
        hbm(ids_t),
        hbm(w_t),
        hbm(tokens),
        hbm(cotangent),
        flops=4 * slots * tok_rows * half * 2,
        far=range(4),
        scratch=landing(ids_t, w_t, tokens, cotangent),
    )
    high, low, right = fused(
        functools.partial(plan_kernel, owners, cap),
        [bf(tok_rows, 2 * slots)] * 3,
        hbm(ids_t),
        hbm(w_t),
        flops=tok_rows**3,
    )

    def trade(rows, axis, *shape):
        return lax.all_to_all(rows.reshape(shape), axis, split_axis=0, concat_axis=0, tiled=True)

    def swap(v):
        return lax.ppermute(v, "tensor", [(0, 1), (1, 0)])

    def pair(v, axis):
        return lax.all_gather(v, axis, axis=1, tiled=True)

    chunks = (owners, 2 * cap, half)
    own = trade(send, "expert", *chunks).reshape(2 * slots, half)
    oth = swap(own)
    floats = jax.ShapeDtypeStruct((slots, ff), F32)
    down_half, in_half = bf(ff, half), bf(half, ff)
    weights = [hbm(w[0]) for w in (gate_weight, up_weight, down_weight)]
    gate, up, cols, wg_oth, wu_oth = fused(
        functools.partial(own_kernel, cap),
        [floats, floats, bf(NX, slots, half // NX), in_half, in_half],
        side,
        own,
        *weights[:2],
        scalars=1,
        flops=slots * half * 2 * ff * 2 + slots * 2 * slots * half * 4,
        mib=12,
        far=(2, 3),
        scratch=[pltpu.VMEM(in_half.shape, B16)] * 2 + [pltpu.SemaphoreType.DMA((4,))],
    )
    gate, up, pack = fused(
        functools.partial(rest_kernel, cap),
        [floats, floats, pltpu.HBM((NX, slots, half // NX + ff), B16)],
        oth,
        gate,
        up,
        cols,
        wg_oth,
        wu_oth,
        flops=slots * half * 2 * ff * 2 + slots * 2 * slots * half * 2,
        mib=12,
        alias={1: 0, 2: 1},
    )
    packs = trade(pack, "x", *pack.shape)
    give, *terms = fused(
        functools.partial(give_kernel, cap),
        [bf(2 * slots, half)] + [bf(slots, ff)] * 3,
        side,
        own,
        oth,
        gate,
        up,
        *weights,
        scalars=1,
        flops=slots * half * 2 * ff * 5 + slots * 2 * slots * half * 8,
        mib=16,
        far=(5, 6, 7),
        scratch=landing(down_half, down_half, in_half, in_half),
    )
    got = swap(give)
    (keep,) = fused(
        functools.partial(keep_kernel, cap),
        [bf(2 * slots, half)],
        side,
        *terms,
        *weights,
        scalars=1,
        flops=slots * half * 2 * ff * 3 + slots * 2 * slots * half * 4,
        mib=12,
        far=(4, 5, 6),
        scratch=landing(down_half, in_half, in_half),
    )
    total = (keep.astype(F32) + got.astype(F32)).astype(B16)
    back = trade(total, "expert", *chunks).reshape(2 * slots, half)
    keep, give = fused(
        down_kernel,
        [bf(2, half // 8, ff)] * 2,
        bits[0],
        packs,
        pair(packs[:, :, : half // NX], "tensor"),
        scalars=1,
        flops=half // 2 * ff * slots * 2 * NX,
    )
    for step, kernel in ((1, halve_rows_kernel), (2, halve_sides_kernel)):
        keep, give = fused(
            kernel,
            [bf(2, keep.shape[1] // 2, ff)] * 2,
            bits[step - 1],
            bits[step],
            keep,
            pair(give, ("y1", "y2")[step - 1]),
            scalars=2,
        )
    mixed, token_grad, down_grad = fused(
        combine_kernel,
        [bf(tok_rows, half)] * 2 + [bf(half // 16, ff)],
        bits[2],
        high,
        low,
        right,
        back,
        keep,
        pair(give, "y4"),
        scalars=1,
        flops=tok_rows * 2 * slots * half * 6,
    )
    return mixed, token_grad, down_grad.T[None]


def solution(mesh):
    dp, owners, tensor = (mesh.shape[a] for a in ("dp", "expert", "tensor"))
    mesh = jax.sharding.Mesh(
        mesh.devices.reshape(2, 2, dp // (4 * NX), NX, owners, tensor),
        ("y4", "y2", "y1", "x", "expert", "tensor"),
    )
    ways = ("y4", "y2", "y1", "x")
    blocks = (*ways, "expert")
    placed = (
        P(blocks, "tensor"),
        P(blocks, None),
        P(blocks, None),
        P("expert", None, "tensor"),
        P("expert", None, "tensor"),
        P("expert", "tensor", None),
        P(blocks, "tensor"),
    )

    return jax.shard_map(
        per_device,
        mesh=mesh,
        in_specs=placed,
        out_specs=(P(blocks, "tensor"), P(blocks, "tensor"), P("expert", "tensor", ways)),
        check_vma=False,
    )
```

```python
import functools
import math

import jax
import jax.numpy as jnp
from jax import lax
from jax.experimental import pallas as pl
from jax.experimental.pallas import tpu as pltpu
from jax.sharding import PartitionSpec as P

EXPERTS = 128
NX = 4
B16 = jnp.bfloat16
F32 = jnp.float32
ROWS0 = (((0,), (0,)), ((), ()))
COLS1 = (((1,), (1,)), ((), ()))


def dot(a, b, dims=None):
    if dims is None:
        dims = (((1,), (0,)), ((), ()))
    return lax.dot_general(a, b, dims, preferred_element_type=F32)


def hbm(v):
    return pltpu.with_memory_space_constraint(v, pltpu.HBM)


def fused(kernel, outs, *args, scalars=0, flops=0, mib=8, far=(), scratch=(), alias=None, blocks=None):
    specs = [
        pl.BlockSpec(
            memory_space=pltpu.SMEM if i < scalars else pltpu.HBM if i in far else pltpu.VMEM
        )
        for i in range(len(args))
    ]
    nbytes = sum(math.prod(a.shape) * a.dtype.itemsize for a in list(args) + list(outs))
    return pl.pallas_call(
        kernel,
        out_shape=outs,
        grid=(1,) if blocks else (),
        in_specs=specs,
        out_specs=[
            (blocks or {}).get(i, pl.BlockSpec(memory_space=pltpu.VMEM)) for i in range(len(outs))
        ],
        scratch_shapes=scratch,
        input_output_aliases=alias or {},
        compiler_params=pltpu.CompilerParams(vmem_limit_bytes=mib << 20),
        cost_estimate=pl.CostEstimate(flops=flops, bytes_accessed=nbytes, transcendentals=0),
    )(*args)


def fetch(pairs, sems):
    copies = [pltpu.make_async_copy(a, b, sems.at[i]) for i, (a, b) in enumerate(pairs)]
    for c in copies:
        c.start()
    return copies


def landing(*shapes):
    return [pltpu.VMEM(v.shape, v.dtype) for v in shapes] + [
        pltpu.SemaphoreType.DMA((len(shapes),))
    ]


def routing(ids_ref, w_ref, owners, cap):
    choose, toks = ids_ref.shape
    expert = lax.broadcasted_iota(jnp.int32, (owners, toks), 0)
    mask = jnp.zeros((owners, toks), F32)
    weight = jnp.zeros((owners, toks), F32)
    for k in range(choose):
        hit = ids_ref[k : k + 1, :] == expert
        mask = mask + jnp.where(hit, 1.0, 0.0)
        weight = weight + jnp.where(hit, w_ref[k : k + 1, :], 0.0)
    earlier = lax.broadcasted_iota(jnp.int32, (toks, toks), 0) < lax.broadcasted_iota(
        jnp.int32, (toks, toks), 1
    )
    rank = dot(mask.astype(B16), jnp.where(earlier, 1.0, 0.0).astype(B16))
    code = jnp.where(mask > 0.0, rank, -100.0)
    shape = (owners, 2 * cap, toks)
    code = jnp.broadcast_to(code[:, None, :], shape)
    weight = jnp.broadcast_to(weight[:, None, :], shape)
    row = lax.broadcasted_iota(jnp.int32, shape, 1).astype(F32)
    flat = (owners * 2 * cap, toks)
    left = jnp.where(code == row, 1.0, 0.0).reshape(flat)
    right = jnp.where(code == row - float(cap), 1.0, 0.0).reshape(flat)
    return left, right, weight.reshape(flat)


def dispatch_kernel(owners, cap, *refs):
    sources, out_ref, landed, sems = refs[:4], refs[4], refs[5:9], refs[9]
    copies = fetch(list(zip(sources, landed, strict=True)), sems)
    ids_ref, w_ref, tok_ref, cot_ref = landed
    copies[0].wait()
    copies[1].wait()
    left, right, weight = routing(ids_ref, w_ref, owners, cap)
    scale = jnp.sum(right * weight, axis=1, keepdims=True)
    left, right = left.astype(B16), right.astype(B16)
    copies[2].wait()
    copies[3].wait()
    out_ref[...] = (dot(left, tok_ref[...]) + dot(right, cot_ref[...]) * scale).astype(B16)


def plan_kernel(owners, cap, ids_ref, w_ref, high_ref, low_ref, right_ref):
    left, right, weight = routing(ids_ref, w_ref, owners, cap)
    left = (left * weight).T
    high = left.astype(B16)
    high_ref[...] = high
    low_ref[...] = (left - high.astype(F32)).astype(B16)
    right_ref[...] = right.T.astype(B16)


def combine_kernel(
    bit_ref, high_ref, low_ref, right_ref, rows_ref, mine_ref, pair_ref, mixed_ref, grad_ref, down_ref
):
    n = mine_ref.shape[1]
    for h in range(2):
        both = mine_ref[h].astype(F32) + partner(bit_ref, pair_ref, h, 0, n)
        down_ref[h * n : (h + 1) * n, :] = both.astype(B16)
    rows = rows_ref[...]
    mixed_ref[...] = (dot(high_ref[...], rows) + dot(low_ref[...], rows)).astype(B16)
    grad_ref[...] = dot(right_ref[...], rows).astype(B16)


def pick(shape, axis, cap, shift):
    compact = lax.broadcasted_iota(jnp.int32, shape, axis).astype(F32)
    chunk = lax.broadcasted_iota(jnp.int32, shape, 1 - axis).astype(F32)
    block = jnp.floor((compact + 0.5) * (1.0 / cap))
    return jnp.where(chunk == compact + cap * block + shift, 1.0, 0.0).astype(B16)


def halves(side_ref, half):
    side = side_ref[0]
    here = pl.ds(pl.multiple_of(side * half, half), half)
    there = pl.ds(pl.multiple_of((1 - side) * half, half), half)
    return side, here, there


def own_kernel(
    cap, side_ref, own_ref, wg_far, wu_far, gate_ref, up_ref, cols_ref, wg_oth, wu_oth, wg, wu, sems
):
    rows, half = own_ref.shape
    slots = rows // 2
    _, here, there = halves(side_ref, half)
    copies = fetch(
        [
            (wg_far.at[here], wg),
            (wu_far.at[here], wu),
            (wg_far.at[there], wg_oth),
            (wu_far.at[there], wu_oth),
        ],
        sems,
    )
    own = own_ref[...]
    x = dot(pick((slots, rows), 0, cap, 0), own).astype(B16)
    g = dot(pick((slots, rows), 0, cap, cap), own).astype(B16)
    wide = half // NX
    for xd in range(NX):
        cols = [g[:, (y * NX + xd) * 64 : (y * NX + xd) * 64 + 64] for y in range(wide // 64)]
        cols_ref[xd, :, 0 : wide // 2] = jnp.concatenate(cols[0::2], axis=1)
        cols_ref[xd, :, wide // 2 : wide] = jnp.concatenate(cols[1::2], axis=1)
    copies[0].wait()
    gate_ref[...] = dot(x, wg[...])
    copies[1].wait()
    up_ref[...] = dot(x, wu[...])
    copies[2].wait()
    copies[3].wait()


def rest_kernel(cap, oth_ref, gate_in, up_in, _, wg_ref, wu_ref, gate_ref, up_ref, pack_ref):
    rows = oth_ref.shape[0]
    slots = rows // 2
    x = dot(pick((slots, rows), 0, cap, 0), oth_ref[...]).astype(B16)
    gate = gate_in[...] + dot(x, wg_ref[...])
    up = up_in[...] + dot(x, wu_ref[...])
    hidden = (gate * (1.0 / (1.0 + jnp.exp(-gate))) * up).astype(B16)
    gate_ref[...] = gate
    up_ref[...] = up
    for xd in range(NX):
        pack_ref[xd] = hidden


def results(cap, hidden, gate_term, up_term, wd, wg, wu):
    slots = hidden.shape[0]
    out_rows = dot(hidden, wd[...]).astype(B16)
    row_grad = (dot(gate_term, wg[...], COLS1) + dot(up_term, wu[...], COLS1)).astype(B16)
    from_x = pick((2 * slots, slots), 1, cap, 0)
    from_g = pick((2 * slots, slots), 1, cap, cap)
    return (dot(from_x, out_rows) + dot(from_g, row_grad)).astype(B16)


def give_kernel(
    cap, side_ref, own_ref, oth_ref, gate_ref, up_ref, wg_far, wu_far, wd_far,
    give_ref, hidden_ref, gate_term_ref, up_term_ref, wd_own, wd_oth, wg, wu, sems,
):
    rows, half = own_ref.shape
    slots = rows // 2
    _, here, there = halves(side_ref, half)
    copies = fetch(
        [
            (wd_far.at[:, here], wd_own),
            (wd_far.at[:, there], wd_oth),
            (wg_far.at[there], wg),
            (wu_far.at[there], wu),
        ],
        sems,
    )
    to_g = pick((slots, rows), 0, cap, cap)
    g_own, g_oth = dot(to_g, own_ref[...]).astype(B16), dot(to_g, oth_ref[...]).astype(B16)
    gate, up = gate_ref[...], up_ref[...]
    sig = 1.0 / (1.0 + jnp.exp(-gate))
    act = gate * sig
    hidden = (act * up).astype(B16)
    copies[0].wait()
    copies[1].wait()
    hidden_grad = dot(g_own, wd_own[...], COLS1) + dot(g_oth, wd_oth[...], COLS1)
    gate_term = (hidden_grad * up * sig * (1.0 + gate * (1.0 - sig))).astype(B16)
    up_term = (hidden_grad * act).astype(B16)
    hidden_ref[...] = hidden
    gate_term_ref[...] = gate_term
    up_term_ref[...] = up_term
    copies[2].wait()
    copies[3].wait()
    give_ref[...] = results(cap, hidden, gate_term, up_term, wd_oth, wg, wu)


def keep_kernel(
    cap, side_ref, hidden_ref, gate_term_ref, up_term_ref, wg_far, wu_far, wd_far,
    keep_ref, wd, wg, wu, sems,
):
    _, here, _ = halves(side_ref, wd.shape[1])
    copies = fetch(
        [(wd_far.at[:, here], wd), (wg_far.at[here], wg), (wu_far.at[here], wu)], sems
    )
    for c in copies:
        c.wait()
    keep_ref[...] = results(cap, hidden_ref[...], gate_term_ref[...], up_term_ref[...], wd, wg, wu)


def down_kernel(bit_ref, packs_ref, cols_ref, keep_ref, give_ref):
    n = keep_ref.shape[1]
    slots = packs_ref.shape[1]
    wide = cols_ref.shape[2]
    bit = bit_ref[0]
    for at, out in ((1 - bit, give_ref), (bit, keep_ref)):
        cols = pl.ds(pl.multiple_of(at * n, n), n)
        for h in range(2):
            total = None
            for k in range(NX):
                rows = cols_ref[k, h * slots : (h + 1) * slots, cols]
                part = dot(rows, packs_ref[k, :, wide:], ROWS0)
                total = part if total is None else total + part
            out[h] = total.astype(B16)


def partner(bit_ref, pair_ref, h, at, n):
    start = (1 - bit_ref[0]) * (pair_ref.shape[1] // 2) + at
    return pair_ref[h, pl.ds(pl.multiple_of(start, n), n), :].astype(F32)


def halve_rows_kernel(last_ref, bit_ref, mine_ref, pair_ref, keep_ref, give_ref):
    n = keep_ref.shape[1]
    bit = bit_ref[0]
    for side, out in ((1 - bit, give_ref), (bit, keep_ref)):
        for h in range(2):
            mine = mine_ref[h, pl.ds(pl.multiple_of(side * n, n), n), :].astype(F32)
            out[h] = (mine + partner(last_ref, pair_ref, h, side * n, n)).astype(B16)


def halve_sides_kernel(last_ref, bit_ref, mine_ref, pair_ref, keep_ref, give_ref):
    n = keep_ref.shape[1]
    bit = bit_ref[0]
    for side, out in ((1 - bit, give_ref), (bit, keep_ref)):
        both = mine_ref[side].astype(F32) + partner(last_ref, pair_ref, side, 0, 2 * n)
        both = both.astype(B16)
        out[0] = both[0:n]
        out[1] = both[n : 2 * n]


def per_device(tokens, expert_ids, route_weight, gate_weight, up_weight, down_weight, cotangent):
    owners = lax.axis_size("expert")
    tok_rows, choose = expert_ids.shape
    cap = 3 * tok_rows * choose // (2 * EXPERTS)
    half = tokens.shape[1]
    slots = owners * cap
    ff = gate_weight.shape[2]
    bf = lambda *shape: jax.ShapeDtypeStruct(shape, B16)
    side = lax.axis_index("tensor").astype(jnp.int32).reshape(1)
    bits = [lax.axis_index(a).astype(jnp.int32).reshape(1) for a in ("y1", "y2", "y4")]
    ids_t, w_t = expert_ids.T, route_weight.T
    (send,) = fused(
        functools.partial(dispatch_kernel, owners, cap),
        [bf(2 * slots, half)],
        hbm(ids_t),
        hbm(w_t),
        hbm(tokens),
        hbm(cotangent),
        flops=4 * slots * tok_rows * half * 2,
        far=range(4),
        scratch=landing(ids_t, w_t, tokens, cotangent),
    )
    high, low, right = fused(
        functools.partial(plan_kernel, owners, cap),
        [bf(tok_rows, 2 * slots)] * 3,
        hbm(ids_t),
        hbm(w_t),
        flops=tok_rows**3,
    )

    def trade(rows, axis, *shape):
        return lax.all_to_all(rows.reshape(shape), axis, split_axis=0, concat_axis=0, tiled=True)

    def swap(v):
        return lax.ppermute(v, "tensor", [(0, 1), (1, 0)])

    def pair(v, axis):
        return lax.all_gather(v, axis, axis=1, tiled=True)

    chunks = (owners, 2 * cap, half)
    own = trade(send, "expert", *chunks).reshape(2 * slots, half)
    oth = swap(own)
    floats = jax.ShapeDtypeStruct((slots, ff), F32)
    down_half, in_half = bf(ff, half), bf(half, ff)
    weights = [hbm(w[0]) for w in (gate_weight, up_weight, down_weight)]
    wide = half // NX
    pack_shape = pltpu.HBM((NX, slots, wide + ff), B16)
    whole = (pl.Element(NX), pl.Element(slots))
    gate, up, pack, wg_oth, wu_oth = fused(
        functools.partial(own_kernel, cap),
        [floats, floats, pack_shape, in_half, in_half],
        side,
        own,
        *weights[:2],
        scalars=1,
        flops=slots * half * 2 * ff * 2 + slots * 2 * slots * half * 4,
        mib=12,
        far=(2, 3),
        scratch=[pltpu.VMEM(in_half.shape, B16)] * 2 + [pltpu.SemaphoreType.DMA((4,))],
        blocks={2: pl.BlockSpec((*whole, pl.Element(wide)), lambda i: (0, 0, 0))},
    )
    gate, up, pack = fused(
        functools.partial(rest_kernel, cap),
        [floats, floats, pack_shape],
        oth,
        gate,
        up,
        pack,
        wg_oth,
        wu_oth,
        flops=slots * half * 2 * ff * 2 + slots * 2 * slots * half * 2,
        mib=12,
        far=(3,),
        alias={1: 0, 2: 1, 3: 2},
        blocks={2: pl.BlockSpec((*whole, pl.Element(ff)), lambda i: (0, 0, wide))},
    )
    packs = trade(pack, "x", *pack.shape)
    give, *terms = fused(
        functools.partial(give_kernel, cap),
        [bf(2 * slots, half)] + [bf(slots, ff)] * 3,
        side,
        own,
        oth,
        gate,
        up,
        *weights,
        scalars=1,
        flops=slots * half * 2 * ff * 5 + slots * 2 * slots * half * 8,
        mib=16,
        far=(5, 6, 7),
        scratch=landing(down_half, down_half, in_half, in_half),
    )
    got = swap(give)
    (keep,) = fused(
        functools.partial(keep_kernel, cap),
        [bf(2 * slots, half)],
        side,
        *terms,
        *weights,
        scalars=1,
        flops=slots * half * 2 * ff * 3 + slots * 2 * slots * half * 4,
        mib=12,
        far=(4, 5, 6),
        scratch=landing(down_half, in_half, in_half),
    )
    total = (keep.astype(F32) + got.astype(F32)).astype(B16)
    back = trade(total, "expert", *chunks).reshape(2 * slots, half)
    keep, give = fused(
        down_kernel,
        [bf(2, half // 8, ff)] * 2,
        bits[0],
        packs,
        pair(packs[:, :, : half // NX], "tensor"),
        scalars=1,
        flops=half // 2 * ff * slots * 2 * NX,
    )
    for step, kernel in ((1, halve_rows_kernel), (2, halve_sides_kernel)):
        keep, give = fused(
            kernel,
            [bf(2, keep.shape[1] // 2, ff)] * 2,
            bits[step - 1],
            bits[step],
            keep,
            pair(give, ("y1", "y2")[step - 1]),
            scalars=2,
        )
    mixed, token_grad, down_grad = fused(
        combine_kernel,
        [bf(tok_rows, half)] * 2 + [bf(half // 16, ff)],
        bits[2],
        high,
        low,
        right,
        back,
        keep,
        pair(give, "y4"),
        scalars=1,
        flops=tok_rows * 2 * slots * half * 6,
    )
    return mixed, token_grad, down_grad.T[None]


def solution(mesh):
    dp, owners, tensor = (mesh.shape[a] for a in ("dp", "expert", "tensor"))
    mesh = jax.sharding.Mesh(
        mesh.devices.reshape(2, 2, dp // (4 * NX), NX, owners, tensor),
        ("y4", "y2", "y1", "x", "expert", "tensor"),
    )
    ways = ("y4", "y2", "y1", "x")
    blocks = (*ways, "expert")
    placed = (
        P(blocks, "tensor"),
        P(blocks, None),
        P(blocks, None),
        P("expert", None, "tensor"),
        P("expert", None, "tensor"),
        P("expert", "tensor", None),
        P(blocks, "tensor"),
    )

    return jax.shard_map(
        per_device,
        mesh=mesh,
        in_specs=placed,
        out_specs=(P(blocks, "tensor"), P(blocks, "tensor"), P("expert", "tensor", ways)),
        check_vma=False,
    )
```
